512 devices in a mesh: wide: 64 (over x, y, core), narrow: 8 (over z).
Axes of the slice: x: 4, y: 8, z: 8, core: 2. Of those that a mesh axis runs over, the one named last changes fastest.
Arguments:
- points: bfloat16 [128, 1024, 512], P('wide', 'narrow'), may hold values from -6 to 6
- counts: int32 [128, 256], P('wide', 'narrow'), may hold values from 1 to 4, as said below
- destination: int32 [128, 256], P('wide', 'narrow'), may hold values from 0 to 63, as said below
- rotated_ball: int32 [128, 256], P('wide', 'narrow'), may hold values from 0 to 1
- qkv_first: bfloat16 [512, 1536], replicated, may hold values from -1 to 1
- out_first: bfloat16 [512, 512], replicated, may hold values from -0.25 to 0.25
- qkv_second: bfloat16 [512, 1536], replicated, may hold values from -1 to 1
- out_second: bfloat16 [512, 512], replicated, may hold values from -0.25 to 0.25
Outputs:
- result: bfloat16 [128, 1024, 512], P('wide', 'narrow')
The draws below stay inside these ranges and needn't reach their ends.
Inputs may be any that keep to these rules, and one draw needn't show every extreme that they name: `counts`: the first block of every ball row has all 4 points usable. Among the blocks of one device, at most 2 have the same destination; on every device some destination receives 2 of its blocks, and some destination receives 2 blocks from every device of its narrow index.
All inputs are finite; a program needn't handle non-finite values.
Results may differ from the reference program's by a relative error of at most 0.0095.
Values may be sent and summed in bfloat16 or wider, within the bound.
A program may use at most 64 MiB of HBM per device.

```python
import math
import jax
import jax.numpy as jnp
from jax import lax

D = 512
HEADS = 8
BALL = 1024
BLK = 4
ROT_BALLS = 2
BALLS_DEV = 2
BALLS = 128
CAP = 2
N_WIDE = 64
N_NARROW = 8


def drawn_weight(key, marker):
    noise = jax.random.normal(jax.random.fold_in(key, marker), (D, 3 * D), jnp.float32)
    weight = jnp.clip(noise, -4.0, 4.0) * (1.0 / math.sqrt(D))
    return weight.astype(jnp.bfloat16)


def draw_points(key, part):
    noise = jax.random.normal(jax.random.fold_in(key, 11), (BALLS, BALL, D), jnp.float32)
    values = jnp.clip(noise, -6.0, 6.0)
    return values.astype(jnp.bfloat16)


def draw_qkv_first(key, part):
    return drawn_weight(key, 21)


def draw_qkv_second(key, part):
    return drawn_weight(key, 31)


def draw_counts(key, part):
    raw_counts = jax.random.randint(key, (BALLS, BALL // BLK), 1, BLK + 1, dtype=jnp.int32)
    return raw_counts.at[:, 0].set(BLK)


def draw_destination(key, part):
    sub_blocks = BALL // N_NARROW // BLK
    block_count = BALLS_DEV * sub_blocks
    slot_total = N_WIDE * CAP
    hotness = jax.random.randint(jax.random.fold_in(key, 1), (N_WIDE,), 0, 8, dtype=jnp.int32)
    hottest = jax.random.randint(jax.random.fold_in(key, 2), (), 0, N_WIDE, dtype=jnp.int32)
    hotness = hotness.at[hottest].set(8)
    hotness = hotness.at[0].set(8)
    hotness = hotness.at[N_WIDE - 1].set(8)
    slot_dest = jnp.arange(slot_total, dtype=jnp.int32) // CAP

    def one_device(device_key):
        noise = jax.random.randint(device_key, (slot_total,), 0, 256, dtype=jnp.int32)
        scores = (hotness[slot_dest] * 256 + noise) * slot_total + jnp.arange(slot_total, dtype=jnp.int32)
        chosen = lax.top_k(scores, block_count)[1]
        picked = slot_dest[chosen]
        order = jax.random.permutation(jax.random.fold_in(device_key, 7), block_count)
        return picked[order]
    device_keys = jax.random.split(jax.random.fold_in(key, 3), N_WIDE * N_NARROW)
    lists = jax.vmap(one_device)(device_keys)
    shaped = lists.reshape(N_WIDE, N_NARROW, BALLS_DEV, sub_blocks)
    return jnp.transpose(shaped, (0, 2, 1, 3)).reshape(BALLS, BALL // BLK).astype(jnp.int32)


def touch_ends(values, key, smallest, high):
    shape = values.shape
    index_at = [jax.random.randint(jax.random.fold_in(key, axis), (), 0, shape[axis]) for axis in range(len(shape))]
    values = values.at[tuple(index_at)].set(smallest)
    longest = shape.index(max(shape))
    index_at[longest] = (index_at[longest] + 1) % shape[longest]
    return values.at[tuple(index_at)].set(high)


def scatter_about(key, extent, spread, reach, kind=jnp.bfloat16):
    values = jax.random.normal(key, extent, jnp.float32) * spread
    return jnp.minimum(jnp.maximum(values, -reach), reach).astype(kind)


def setup_inputs(seed: int = 0) -> dict:
    arg_keys = jax.random.split(jax.random.key(seed), 9)
    return {
        "points": draw_points(jax.random.fold_in(arg_keys[8], 71), 0),
        "counts": draw_counts(jax.random.fold_in(arg_keys[8], 71), 0),
        "destination": draw_destination(jax.random.fold_in(arg_keys[8], 71), 0),
        "rotated_ball": touch_ends(jax.random.randint(arg_keys[3], (BALLS, BALL // BLK), 0, ROT_BALLS), jax.random.fold_in(arg_keys[3], 1), 0, ROT_BALLS - 1).astype(jnp.int32),
        "qkv_first": draw_qkv_first(jax.random.fold_in(arg_keys[8], 71), 0),
        "out_first": scatter_about(arg_keys[5], (D, D), D ** -0.5, 0.25),
        "qkv_second": draw_qkv_second(jax.random.fold_in(arg_keys[8], 71), 0),
        "out_second": scatter_about(arg_keys[7], (D, D), D ** -0.5, 0.25),
    }


EPSILON = 1e-06
NEGATIVE = -1e+30

def rms_round(values):
    widened = values.astype(jnp.float32)
    scaled = widened * lax.rsqrt(lax.optimization_barrier(jnp.mean(widened * widened, axis=-1, keepdims=True)) + EPSILON)
    return scaled.astype(jnp.bfloat16)

def project(normed, weight):
    flat = normed.reshape(-1, normed.shape[-1])
    product = jnp.dot(flat, weight, preferred_element_type=jnp.float32)
    return product.reshape(normed.shape[:-1] + (weight.shape[1],))

def split_heads(block_rows, offset, model_width):
    head_dim = model_width // HEADS
    return block_rows[..., offset:offset + model_width].reshape(block_rows.shape[:-1] + (HEADS, head_dim)).astype(jnp.float32)

def usable_points(counts):
    position = lax.broadcasted_iota(jnp.int32, counts.shape + (BLK,), len(counts.shape))
    usable = position < counts[..., None]
    return usable.reshape(counts.shape[:-1] + (counts.shape[-1] * BLK,))

def pool_rows(qkv_all, counts):
    model_width = qkv_all.shape[-1] // 3
    usable = usable_points(counts)
    kv_part = qkv_all[..., model_width:].astype(jnp.float32) * usable[..., None].astype(jnp.float32)
    grouped = kv_part.reshape(counts.shape + (BLK, 2 * model_width)).sum(axis=-2)
    return (grouped / counts[..., None].astype(jnp.float32)).astype(jnp.bfloat16)

def fine_coarse(ball_qkv, fine_usable, coarse_kv):
    model_width = coarse_kv.shape[-1] // 2
    scaling = 1.0 / math.sqrt(model_width // HEADS)
    queries = split_heads(ball_qkv, 0, model_width)
    key_fine = split_heads(ball_qkv, model_width, model_width)
    value_fine = split_heads(ball_qkv, 2 * model_width, model_width)
    key_coarse = split_heads(coarse_kv, 0, model_width)
    value_coarse = split_heads(coarse_kv, model_width, model_width)
    score_fine = jnp.einsum('qhe,khe->hqk', queries, key_fine) * scaling
    score_fine = jnp.where(fine_usable[None, None, :], score_fine, NEGATIVE)
    score_coarse = jnp.einsum('qhe,khe->hqk', queries, key_coarse) * scaling
    highest = jnp.maximum(lax.optimization_barrier(jnp.max(score_fine, axis=-1)), lax.optimization_barrier(jnp.max(score_coarse, axis=-1)))[..., None]
    exp_fine = jnp.exp(score_fine - highest)
    exp_coarse = jnp.exp(score_coarse - highest)
    denominator = lax.optimization_barrier(jnp.sum(exp_fine, axis=-1, keepdims=True)) + lax.optimization_barrier(jnp.sum(exp_coarse, axis=-1, keepdims=True))
    weight_fine = (exp_fine / denominator).astype(jnp.bfloat16).astype(jnp.float32)
    weight_coarse = (exp_coarse / denominator).astype(jnp.bfloat16).astype(jnp.float32)
    mixture = jnp.einsum('hqk,khe->qhe', weight_fine, value_fine) + jnp.einsum('hqk,khe->qhe', weight_coarse, value_coarse)
    return mixture.reshape(mixture.shape[0], model_width).astype(jnp.bfloat16)

def ball_attention(recv_rows, row_ball, row_usable):
    total_rows = recv_rows.shape[0]
    model_width = recv_rows.shape[1] // 3
    scaling = 1.0 / math.sqrt(model_width // HEADS)
    queries = split_heads(recv_rows, 0, model_width)
    key_rows = split_heads(recv_rows, model_width, model_width)
    value_rows = split_heads(recv_rows, 2 * model_width, model_width)
    block_len = min(256, total_rows)

    def one_block(block_idx):
        offset = (block_idx * block_len).astype(jnp.int32)
        query_block = lax.dynamic_slice_in_dim(queries, offset, block_len, 0)
        ball_block = lax.dynamic_slice_in_dim(row_ball, offset, block_len, 0)
        scores = jnp.einsum('qhe,khe->hqk', query_block, key_rows) * scaling
        allowed = (ball_block[:, None] == row_ball[None, :]) & row_usable[None, :]
        scores = jnp.where(allowed[None], scores, NEGATIVE)
        highest = lax.optimization_barrier(jnp.max(scores, axis=-1, keepdims=True))
        exponent = jnp.exp(scores - highest)
        weights = (exponent / lax.optimization_barrier(jnp.sum(exponent, axis=-1, keepdims=True))).astype(jnp.bfloat16).astype(jnp.float32)
        mixture = jnp.einsum('hqk,khe->qhe', weights, value_rows)
        return mixture.reshape(block_len, model_width).astype(jnp.bfloat16)
    blocks_out = lax.map(one_block, jnp.arange(total_rows // block_len, dtype=jnp.int32))
    return blocks_out.reshape(total_rows, model_width)

def by_source(array_in, sub_blocks):
    rest = array_in.shape[2:]
    shaped = array_in.reshape((N_WIDE, BALLS_DEV, N_NARROW, sub_blocks) + rest)
    moved = jnp.moveaxis(shaped, 2, 0)
    return moved.reshape((N_NARROW, N_WIDE, BALLS_DEV * sub_blocks) + rest)

def from_source(array_in, sub_blocks):
    rest = array_in.shape[3:]
    shaped = array_in.reshape((N_NARROW, N_WIDE, BALLS_DEV, sub_blocks) + rest)
    moved = jnp.moveaxis(shaped, 0, 2)
    return moved.reshape((BALLS, N_NARROW * sub_blocks) + rest)

def reference(points, counts, destination, rotated_ball, qkv_first, out_first, qkv_second, out_second):
    model_width = points.shape[-1]
    share = BALL // N_NARROW
    sub_blocks = share // BLK
    normed_one = rms_round(points)
    qkv_one = project(normed_one, qkv_first).astype(jnp.bfloat16)
    pooled = pool_rows(qkv_one, counts)
    usable = usable_points(counts)

    def per_ball(ball_idx):
        ball_qkv = qkv_one[ball_idx].reshape(N_NARROW, share, 3 * model_width)
        ball_usable = usable[ball_idx].reshape(N_NARROW, share)
        attended = jax.vmap(fine_coarse, in_axes=(0, 0, None))(ball_qkv, ball_usable, pooled[ball_idx])
        return attended.reshape(BALL, model_width)
    attended_one = lax.map(per_ball, jnp.arange(BALLS, dtype=jnp.int32))
    layer_one = (points.astype(jnp.float32) + project(attended_one, out_first)).astype(jnp.bfloat16)
    normed_two = rms_round(layer_one)
    qkv_two = project(normed_two, qkv_second).astype(jnp.bfloat16)
    qkv_source = by_source(qkv_two.reshape(BALLS, BALL // BLK, BLK, 3 * model_width), sub_blocks)
    dest_source = by_source(destination, sub_blocks)
    ball_source = by_source(rotated_ball, sub_blocks)
    count_source = by_source(counts, sub_blocks)
    onehot = (dest_source[..., None] == jnp.arange(N_WIDE, dtype=jnp.int32)).astype(jnp.int32)
    earlier = jnp.cumsum(onehot, axis=2, dtype=jnp.int32) - onehot
    rank_in = lax.optimization_barrier(jnp.sum(earlier * onehot, axis=-1, dtype=jnp.int32))
    narrow_idx = lax.broadcasted_iota(jnp.int32, dest_source.shape, 0)
    wide_idx = lax.broadcasted_iota(jnp.int32, dest_source.shape, 1)
    block_idx = lax.broadcasted_iota(jnp.int32, dest_source.shape, 2)
    table = jnp.full((N_NARROW, N_WIDE, N_WIDE, CAP), -1, jnp.int32)
    table = table.at[narrow_idx, dest_source, wide_idx, rank_in].set(block_idx)
    sources = jnp.arange(N_WIDE, dtype=jnp.int32)[:, None]

    def receive(pair):
        narrow_at = pair // N_WIDE
        recv_at = pair % N_WIDE
        picks = table[narrow_at, recv_at]
        live = picks >= 0
        safe_pick = jnp.maximum(picks, 0)
        block_rows = qkv_source[narrow_at][sources, safe_pick]
        block_rows = jnp.where(live[..., None, None], block_rows, jnp.zeros_like(block_rows))
        ball_ids = jnp.where(live, ball_source[narrow_at][sources, safe_pick], -1)
        fill_in = jnp.where(live, count_source[narrow_at][sources, safe_pick], 0)
        row_ball = jnp.broadcast_to(ball_ids[..., None], ball_ids.shape + (BLK,)).reshape(-1)
        row_usable = usable_points(fill_in).reshape(-1)
        return ball_attention(block_rows.reshape(-1, 3 * model_width), row_ball, row_usable)
    received = lax.map(receive, jnp.arange(N_NARROW * N_WIDE, dtype=jnp.int32))
    received = received.reshape(N_NARROW, N_WIDE, N_WIDE, CAP, BLK, model_width)
    back_source = received[narrow_idx, dest_source, wide_idx, rank_in]
    attended_two = from_source(back_source, sub_blocks).reshape(BALLS, BALL, model_width)
    return (layer_one.astype(jnp.float32) + project(attended_two, out_second)).astype(jnp.bfloat16)
```

```python
import functools
import math

import jax
import jax.numpy as jnp
from jax import lax
from jax.experimental import pallas as pl
from jax.experimental.pallas import tpu as pltpu
from jax.sharding import PartitionSpec as P

HEADS = 8
BLK = 4
NX, NY, NZ = 4, 8, 8
WIDE = 2 * NX * NY
ROWS = 256
BLOCKS = 64
SHARE = 128
WIDTH = 512
SLOT = 2 * BLK
SLOTROWS = WIDE * SLOT
PAIRS = HEADS // 2
DY = (0, 4, 1, 7, 2, 6, 3, 5)
GROUPS = 4
GSLOTS = WIDE // GROUPS
GROWS = GSLOTS * SLOT

EPSILON = 1e-06
NEGATIVE = -1e30
MESH = pl.DeviceIdType.MESH
F32 = jnp.float32
BF16 = jnp.bfloat16


def iota(shape, axis):
    return lax.broadcasted_iota(jnp.int32, shape, axis)


def rms_round(values):
    scaled = values * lax.rsqrt(jnp.mean(values * values, axis=-1, keepdims=True) + EPSILON)
    return scaled.astype(BF16)


def dot(left, right):
    return jnp.dot(left, right, preferred_element_type=F32)


def dot_t(left, right):
    return lax.dot_general(left, right, (((1,), (1,)), ((), ())), preferred_element_type=F32)


def column(ref, rows, per):
    values = ref[...].astype(F32)
    half = values.shape[1]
    block = iota((rows, half), 0) // per
    lane = iota((rows, half), 1)
    first = jnp.where(block == lane, values[0:1, :], 0.0)
    second = jnp.where(block == lane + half, values[1:2, :], 0.0)
    return jnp.sum(first + second, axis=1, keepdims=True)


def to_lanes(col):
    rows = col.shape[0]
    eye = iota((rows, rows), 0) == iota((rows, rows), 1)
    return jnp.sum(jnp.where(eye, col, 0.0), axis=0, keepdims=True)


def two_heads(pair):
    low = iota(pair.shape, 1) < 64
    zero = jnp.zeros_like(pair)
    return jnp.concatenate([jnp.where(low, pair, zero), jnp.where(low, zero, pair)], axis=0)


def softmax_values(scores, values):
    highest = jnp.max(scores, axis=1, keepdims=True)
    weights = jnp.exp(scores - highest).astype(BF16)
    ones = jnp.ones((values.shape[0], 128), BF16)
    mixed = dot(weights, jnp.concatenate([values, ones], axis=1))
    mixed = mixed[:, :128] / mixed[:, 128:]
    half = mixed.shape[0] // 2
    low = iota((half, 128), 1) < 64
    return jnp.where(low, mixed[:half], mixed[half:])


def kernel(
    pts_h, cnt_h, dst_h, rot_h, w1_h, o1_h, w2_h, o2_h,
    out_ref,
    pts, cnt, dst, rot, w1, o1, w2, o2,
    ag, meta_s, meta_r, snd, rcv, bsnd, brcv, qkv1, qkv2, unpack,
    load_sem, ring_send, ring_recv, meta_send, meta_recv, fwd_send, fwd_recv, back_send, back_recv,
):
    wide = lax.axis_index("wide")
    z = lax.axis_index("narrow")
    x_me = wide // (2 * NY)
    y_me = (wide // 2) % NY
    c_me = wide % 2

    loads = [
        pltpu.make_async_copy(src, dest, load_sem.at[i])
        for i, (src, dest) in enumerate(
            ((cnt_h, cnt), (dst_h, dst), (rot_h, rot), (pts_h, pts), (w1_h, w1), (o1_h, o1), (w2_h, w2), (o2_h, o2))
        )
    ]
    for load in loads:
        load.start()

    def peer(dy, i):
        return ((x_me + i // 2) % NX) * (2 * NY) + ((y_me + dy) % NY) * 2 + (c_me + i) % 2

    def source(dy, i):
        return ((x_me + NX - i // 2) % NX) * (2 * NY) + ((y_me + NY - dy) % NY) * 2 + (c_me + i) % 2

    def each_slot(visit, groups=range(GROUPS)):
        for g in groups:
            for h in range(2):
                j = 2 * g + h

                def one(i, carry, j=j, g=g):
                    visit(8 * j + i, g, DY[j], i)
                    return carry

                lax.fori_loop(1 if j == 0 else 0, 8, one, 0)

    barrier = pltpu.get_barrier_semaphore()
    up, down = (z + 1) % NZ, (z + NZ - 1) % NZ
    for other in (up, down):
        pl.semaphore_signal(barrier, inc=1, device_id=(wide, other), device_id_type=MESH)

    def greet(k, g, dy, i):
        pl.semaphore_signal(barrier, inc=1, device_id=(peer(dy, i), z), device_id_type=MESH)

    each_slot(greet)

    loads[0].wait()
    cnt64 = column(cnt, BLOCKS, 1)
    r_b, r_l = iota((BLOCKS, ROWS), 0), iota((BLOCKS, ROWS), 1)
    pool = (r_l // BLK == r_b) & ((r_l % BLK).astype(F32) < cnt64)
    pool = jnp.where(pool, 1.0, 0.0).astype(BF16)
    loads[3].wait()
    normed_one = rms_round(pts[...].astype(F32))
    pooled = (dot(pool, normed_one) / cnt64).astype(BF16)
    ag[0] = pooled.reshape(2, BLOCKS // 2, WIDTH)

    pl.semaphore_wait(barrier, WIDE - 1 + 2)

    def hop(way, step, ball):
        here = (step if way == 0 else (NZ - step) % NZ)
        there = step + 1 if way == 0 else NZ - 1 - step
        return pltpu.make_async_remote_copy(
            src_ref=ag.at[here, ball],
            dst_ref=ag.at[there, ball],
            send_sem=ring_send.at[way, step, ball],
            recv_sem=ring_recv.at[there, ball],
            device_id=(wide, up if way == 0 else down),
            device_id_type=MESH,
        )

    sent = []

    def ring(step):
        for ball in range(2):
            for way in range(2):
                if step == 3 and ball != way:
                    continue
                if step > 0:
                    hop(way, step - 1, ball).wait_recv()
                copy = hop(way, step, ball)
                copy.start()
                sent.append(copy)

    ring(0)

    loads[1].wait()
    loads[2].wait()
    cnt_col = column(cnt, ROWS, BLK)
    rot_col = column(rot, ROWS, BLK)
    dst_col = column(dst, ROWS, BLK)
    q_r, q_l = iota((ROWS, ROWS), 0), iota((ROWS, ROWS), 1)
    same = (dst_col == to_lanes(dst_col)) & (q_l // BLK < q_r // BLK)
    rank = jnp.sum(jnp.where(same, 1.0 / BLK, 0.0), axis=1, keepdims=True)
    dst_i = dst_col.astype(jnp.int32)
    d_x = ((dst_i // (2 * NY)) + NX - x_me) % NX
    d_y = ((dst_i // 2) % NY + NY - y_me) % NY
    d_c = (dst_i + c_me) % 2
    turn = jnp.where(d_y < 4, 2 * d_y, (17 - 2 * d_y) % 8)
    slot = (8 * turn + 2 * d_x + d_c) * SLOT + iota((ROWS, 1), 0) % BLK
    slot_col = slot.astype(F32) + rank * BLK
    slot_lane = to_lanes(slot_col)
    unpack[...] = jnp.where(iota((ROWS, SLOTROWS), 1).astype(F32) == slot_col, 1.0, 0.0).astype(BF16)
    pack = jnp.where(iota((SLOTROWS, ROWS), 0).astype(F32) == slot_lane, 1.0, 0.0).astype(BF16)

    ring(1)

    in_first = jnp.where(rot_col == 0.0, 1.0, 0.0)
    usable = jnp.where((iota((ROWS, 1), 0) % BLK).astype(F32) < cnt_col, 1.0, 0.0)
    lane = iota((ROWS, 128), 1)
    meta = jnp.where(lane == 0, in_first, 0.0)
    meta = jnp.where(lane == 1, 1.0 - in_first, meta)
    meta = jnp.where(lane == 2, in_first * usable, meta)
    meta = jnp.where(lane == 3, (1.0 - in_first) * usable, meta)
    meta_slots = dot(pack, meta.astype(BF16)).reshape(WIDE, SLOT, 128).astype(BF16)
    meta_s[...] = meta_slots
    meta_r[0] = meta_slots[0]

    def move(src, dest, k, send_sem, recv_sem, to):
        return pltpu.make_async_remote_copy(
            src_ref=src.at[k],
            dst_ref=dest.at[k],
            send_sem=send_sem,
            recv_sem=recv_sem,
            device_id=(to, z),
            device_id_type=MESH,
        )

    def send_meta(k, g, dy, i):
        move(meta_s, meta_r, k, meta_send, meta_recv, peer(dy, i)).start()

    each_slot(send_meta)

    loads[4].wait()
    qkv1[...] = dot(normed_one, w1[...]).astype(BF16)
    ring(2)
    bias = jnp.where(to_lanes(usable) > 0.0, 0.0, NEGATIVE)
    ring(3)
    for ball in range(2):
        hop(0, 2, 1 - ball).wait_recv() if ball == 0 else hop(1, 2, 1 - ball).wait_recv()
    hop(0, 3, 0).wait_recv()
    hop(1, 3, 1).wait_recv()

    attended = []
    for ball in range(2):
        pooled_all = ag[:, ball].reshape(NZ * BLOCKS // 2, WIDTH)
        pooled_kv = dot(pooled_all, w1[:, WIDTH:]).astype(BF16)
        mine = pl.ds(ball * SHARE, SHARE)
        bias_ball = jnp.concatenate(
            [bias[:, ball * SHARE : (ball + 1) * SHARE], jnp.zeros((1, NZ * BLOCKS // 2), F32)], axis=1
        )
        parts = []
        for pair in range(PAIRS):
            at = pair * 128
            query = two_heads(qkv1[mine, at : at + 128] * 0.125)
            key = jnp.concatenate(
                [qkv1[mine, WIDTH + at : WIDTH + at + 128], pooled_kv[:, at : at + 128]], axis=0
            )
            value = jnp.concatenate(
                [
                    qkv1[mine, 2 * WIDTH + at : 2 * WIDTH + at + 128],
                    pooled_kv[:, WIDTH + at : WIDTH + at + 128],
                ],
                axis=0,
            )
            parts.append(softmax_values(dot_t(query, key) + bias_ball, value).astype(BF16))
        attended.append(jnp.concatenate(parts, axis=1))
    attended_one = jnp.concatenate(attended, axis=0)
    loads[5].wait()
    layer_one = (pts[...].astype(F32) + dot(attended_one, o1[...])).astype(BF16)
    pts[...] = layer_one
    normed_two = rms_round(layer_one.astype(F32))
    slots = dot(pack, normed_two).reshape(WIDE, SLOT, WIDTH).astype(BF16)
    snd[...] = slots
    rcv[0] = slots[0]

    def send_rows(k, g, dy, i):
        move(snd, rcv, k, fwd_send, fwd_recv.at[g], peer(dy, i)).start()

    each_slot(send_rows)

    def arrived(src, dest, first, count, send_sem, recv_sem):
        return pltpu.make_async_remote_copy(
            src_ref=src.at[pl.ds(first, count)],
            dst_ref=dest.at[pl.ds(first, count)],
            send_sem=send_sem,
            recv_sem=recv_sem,
            device_id=(peer(0, 1), z),
            device_id_type=MESH,
        )

    def group(g):
        return (1, GSLOTS - 1) if g == 0 else (g * GSLOTS, GSLOTS)

    arrived(meta_s, meta_r, 1, WIDE - 1, meta_send, meta_recv).wait_recv()
    marks = meta_r[...].astype(F32).reshape(SLOTROWS, 128)
    lanes = iota((SLOTROWS, 128), 1)
    use = (lanes == 2) | (lanes == 3)
    query_mark = jnp.where(use, pltpu.roll(marks, 2, 1), 0.0).astype(BF16)
    key_mark = jnp.where(use, (1.0 - marks) * NEGATIVE, 0.0).astype(BF16)

    loads[6].wait()
    for g in range(GROUPS):
        first, count = group(g)
        arrived(snd, rcv, first, count, fwd_send, fwd_recv.at[g]).wait_recv()
        rows = rcv[g * GSLOTS : (g + 1) * GSLOTS].astype(F32).reshape(GROWS, WIDTH).astype(BF16)
        qkv2[g * GROWS : (g + 1) * GROWS, :] = dot(rows, w2[...]).astype(BF16)

    for g in range(GROUPS):
        mine = slice(g * GROWS, (g + 1) * GROWS)
        mark = query_mark[mine]
        parts = []
        for pair in range(PAIRS):
            at = pair * 128
            query = two_heads(qkv2[mine, at : at + 128] * 0.125)
            query = jnp.concatenate([query, jnp.concatenate([mark, mark], axis=0)], axis=1)
            key = jnp.concatenate([qkv2[:, WIDTH + at : WIDTH + at + 128], key_mark], axis=1)
            value = qkv2[:, 2 * WIDTH + at : 2 * WIDTH + at + 128]
            parts.append(softmax_values(dot_t(query, key), value))
        mixture = jnp.concatenate(parts, axis=1).reshape(GSLOTS, SLOT, WIDTH).astype(BF16)
        bsnd[g * GSLOTS : (g + 1) * GSLOTS] = mixture
        if g == 0:
            brcv[0] = mixture[0]

        def send_back(k, g, dy, i):
            move(bsnd, brcv, k, back_send, back_recv.at[g], source(dy, i)).start()

        each_slot(send_back, (g,))

    loads[7].wait()
    total = jnp.zeros((ROWS, WIDTH), F32)
    for g in range(GROUPS):
        first, count = group(g)
        arrived(bsnd, brcv, first, count, back_send, back_recv.at[g]).wait_recv()
        rows = brcv[g * GSLOTS : (g + 1) * GSLOTS].astype(F32).reshape(GROWS, WIDTH).astype(BF16)
        total = total + dot(unpack[:, g * GROWS : (g + 1) * GROWS], rows)
    out_ref[...] = (pts[...].astype(F32) + dot(total.astype(BF16), o2[...])).astype(BF16)

    for copy in sent:
        copy.wait_send()
    arrived(meta_s, meta_r, 1, WIDE - 1, meta_send, meta_recv).wait_send()
    arrived(snd, rcv, 1, WIDE - 1, fwd_send, fwd_recv.at[0]).wait_send()
    arrived(bsnd, brcv, 1, WIDE - 1, back_send, back_recv.at[0]).wait_send()


def on_device(points, counts, destination, rotated_ball, qkv_first, out_first, qkv_second, out_second):
    rows = points.reshape(ROWS, WIDTH)
    dma = pltpu.SemaphoreType.DMA
    hbm = pl.BlockSpec(memory_space=pltpu.MemorySpace.HBM)
    result = pl.pallas_call(
        kernel,
        out_shape=jax.ShapeDtypeStruct((ROWS, WIDTH), BF16),
        in_specs=[hbm] * 8,
        out_specs=pl.BlockSpec(memory_space=pltpu.VMEM),
        scratch_shapes=[
            pltpu.VMEM((ROWS, WIDTH), BF16),
            pltpu.VMEM((2, 32), jnp.int32),
            pltpu.VMEM((2, 32), jnp.int32),
            pltpu.VMEM((2, 32), jnp.int32),
            pltpu.VMEM((WIDTH, 3 * WIDTH), BF16),
            pltpu.VMEM((WIDTH, WIDTH), BF16),
            pltpu.VMEM((WIDTH, 3 * WIDTH), BF16),
            pltpu.VMEM((WIDTH, WIDTH), BF16),
            pltpu.VMEM((NZ, 2, BLOCKS // 2, WIDTH), BF16),
            pltpu.VMEM((WIDE, SLOT, 128), BF16),
            pltpu.VMEM((WIDE, SLOT, 128), BF16),
            pltpu.VMEM((WIDE, SLOT, WIDTH), BF16),
            pltpu.VMEM((WIDE, SLOT, WIDTH), BF16),
            pltpu.VMEM((WIDE, SLOT, WIDTH), BF16),
            pltpu.VMEM((WIDE, SLOT, WIDTH), BF16),
            pltpu.VMEM((ROWS, 3 * WIDTH), BF16),
            pltpu.VMEM((SLOTROWS, 3 * WIDTH), BF16),
            pltpu.VMEM((ROWS, SLOTROWS), BF16),
            dma((8,)),
            dma((2, 4, 2)),
            dma((NZ, 2)),
            dma,
            dma,
            dma,
            dma((GROUPS,)),
            dma,
            dma((GROUPS,)),
        ],
        compiler_params=pltpu.CompilerParams(
            collective_id=0, has_side_effects=True, vmem_limit_bytes=48 * 1024 * 1024
        ),
    )(rows, counts, destination, rotated_ball, qkv_first, out_first, qkv_second, out_second)
    return result.reshape(points.shape)


def solution(mesh):
    in_specs = (
        P("wide", "narrow", None),
        P("wide", "narrow"),
        P("wide", "narrow"),
        P("wide", "narrow"),
        P(),
        P(),
        P(),
        P(),
    )
    out_specs = P("wide", "narrow", None)
    return jax.shard_map(
        on_device, mesh=mesh, in_specs=in_specs, out_specs=out_specs, check_vma=False
    )
```

```python
import functools
import math

import jax
import jax.numpy as jnp
from jax import lax
from jax.experimental import pallas as pl
from jax.experimental.pallas import tpu as pltpu
from jax.sharding import PartitionSpec as P

HEADS = 8
BLK = 4
NX, NY, NZ = 4, 8, 8
WIDE = 2 * NX * NY
ROWS = 256
BLOCKS = 64
SHARE = 128
WIDTH = 512
SLOT = 2 * BLK
SLOTROWS = WIDE * SLOT
PAIRS = HEADS // 2
DY = (0, 4, 1, 7, 2, 6, 3, 5)
GROUPS = 4
GSLOTS = WIDE // GROUPS
GROWS = GSLOTS * SLOT

EPSILON = 1e-06
NEGATIVE = -1e30
MESH = pl.DeviceIdType.MESH
F32 = jnp.float32
BF16 = jnp.bfloat16


def iota(shape, axis):
    return lax.broadcasted_iota(jnp.int32, shape, axis)


def rms_round(values):
    scaled = values * lax.rsqrt(jnp.mean(values * values, axis=-1, keepdims=True) + EPSILON)
    return scaled.astype(BF16)


def dot(left, right):
    return jnp.dot(left, right, preferred_element_type=F32)


def dot_t(left, right):
    return lax.dot_general(left, right, (((1,), (1,)), ((), ())), preferred_element_type=F32)


def column(ref, rows, per):
    values = ref[...].astype(F32)
    half = values.shape[1]
    block = iota((rows, half), 0) // per
    lane = iota((rows, half), 1)
    first = jnp.where(block == lane, values[0:1, :], 0.0)
    second = jnp.where(block == lane + half, values[1:2, :], 0.0)
    return jnp.sum(first + second, axis=1, keepdims=True)


def to_lanes(col):
    rows = col.shape[0]
    eye = iota((rows, rows), 0) == iota((rows, rows), 1)
    return jnp.sum(jnp.where(eye, col, 0.0), axis=0, keepdims=True)


def two_heads(pair):
    low = iota(pair.shape, 1) < 64
    zero = jnp.zeros_like(pair)
    return jnp.concatenate([jnp.where(low, pair, zero), jnp.where(low, zero, pair)], axis=0)


def softmax_values(scores, values):
    highest = jnp.max(scores, axis=1, keepdims=True)
    weights = jnp.exp(scores - highest).astype(BF16)
    ones = jnp.ones((values.shape[0], 128), BF16)
    mixed = dot(weights, jnp.concatenate([values, ones], axis=1))
    mixed = mixed[:, :128] / mixed[:, 128:]
    half = mixed.shape[0] // 2
    low = iota((half, 128), 1) < 64
    return jnp.where(low, mixed[:half], mixed[half:])


def kernel(
    pts_h, cnt_h, dst_h, rot_h, w1_h, o1_h, w2_h, o2_h,
    out_ref,
    pts, cnt, dst, rot, w1, o1, w2, o2,
    ag, meta_s, meta_r, snd, rcv, bsnd, brcv, qkv1, qkv2, unpack,
    load_sem, ring_send, ring_recv, meta_send, meta_recv, fwd_send, fwd_recv, back_send, back_recv,
):
    wide = lax.axis_index("wide")
    z = lax.axis_index("narrow")
    x_me = wide // (2 * NY)
    y_me = (wide // 2) % NY
    c_me = wide % 2

    loads = [
        pltpu.make_async_copy(src, dest, load_sem.at[i])
        for i, (src, dest) in enumerate(
            ((cnt_h, cnt), (dst_h, dst), (rot_h, rot), (pts_h, pts), (w1_h, w1), (o1_h, o1), (w2_h, w2), (o2_h, o2))
        )
    ]
    for i in (3, 0, 1, 2, 4):
        loads[i].start()

    def peer(dy, i):
        return ((x_me + i // 2) % NX) * (2 * NY) + ((y_me + dy) % NY) * 2 + (c_me + i) % 2

    def source(dy, i):
        return ((x_me + NX - i // 2) % NX) * (2 * NY) + ((y_me + NY - dy) % NY) * 2 + (c_me + i) % 2

    def each_slot(visit, groups=range(GROUPS)):
        for g in groups:
            for h in range(2):
                j = 2 * g + h

                for i in range(1 if j == 0 else 0, 8):
                    visit(8 * j + i, g, DY[j], i)

    barrier = pltpu.get_barrier_semaphore()
    up, down = (z + 1) % NZ, (z + NZ - 1) % NZ
    for other in (up, down):
        pl.semaphore_signal(barrier, inc=1, device_id=(wide, other), device_id_type=MESH)

    def greet(k, g, dy, i):
        pl.semaphore_signal(barrier, inc=1, device_id=(peer(dy, i), z), device_id_type=MESH)

    each_slot(greet)

    loads[0].wait()
    cnt64 = column(cnt, BLOCKS, 1)
    r_b, r_l = iota((BLOCKS, ROWS), 0), iota((BLOCKS, ROWS), 1)
    pool = (r_l // BLK == r_b) & ((r_l % BLK).astype(F32) < cnt64)
    pool = jnp.where(pool, 1.0, 0.0).astype(BF16)
    loads[3].wait()
    normed_one = rms_round(pts[...].astype(F32))
    pooled = (dot(pool, normed_one) / cnt64).astype(BF16)
    ag[0] = pooled.reshape(2, BLOCKS // 2, WIDTH)

    pl.semaphore_wait(barrier, WIDE - 1 + 2)

    def hop(way, step, ball):
        here = (step if way == 0 else (NZ - step) % NZ)
        there = step + 1 if way == 0 else NZ - 1 - step
        return pltpu.make_async_remote_copy(
            src_ref=ag.at[here, ball],
            dst_ref=ag.at[there, ball],
            send_sem=ring_send.at[way, step, ball],
            recv_sem=ring_recv.at[there, ball],
            device_id=(wide, up if way == 0 else down),
            device_id_type=MESH,
        )

    sent = []

    def ring(step):
        for ball in range(2):
            for way in range(2):
                if step == 3 and ball != way:
                    continue
                if step > 0:
                    hop(way, step - 1, ball).wait_recv()
                copy = hop(way, step, ball)
                copy.start()
                sent.append(copy)

    ring(0)
    for i in (5, 6, 7):
        loads[i].start()

    loads[1].wait()
    loads[2].wait()
    cnt_col = column(cnt, ROWS, BLK)
    rot_col = column(rot, ROWS, BLK)
    dst_col = column(dst, ROWS, BLK)
    q_r, q_l = iota((ROWS, ROWS), 0), iota((ROWS, ROWS), 1)
    same = (dst_col == to_lanes(dst_col)) & (q_l // BLK < q_r // BLK)
    rank = jnp.sum(jnp.where(same, 1.0 / BLK, 0.0), axis=1, keepdims=True)
    dst_i = dst_col.astype(jnp.int32)
    d_x = ((dst_i // (2 * NY)) + NX - x_me) % NX
    d_y = ((dst_i // 2) % NY + NY - y_me) % NY
    d_c = (dst_i + c_me) % 2
    turn = jnp.where(d_y < 4, 2 * d_y, (17 - 2 * d_y) % 8)
    slot = (8 * turn + 2 * d_x + d_c) * SLOT + iota((ROWS, 1), 0) % BLK
    slot_col = slot.astype(F32) + rank * BLK
    slot_lane = to_lanes(slot_col)
    unpack[...] = jnp.where(iota((ROWS, SLOTROWS), 1).astype(F32) == slot_col, 1.0, 0.0).astype(BF16)
    pack = jnp.where(iota((SLOTROWS, ROWS), 0).astype(F32) == slot_lane, 1.0, 0.0).astype(BF16)

    ring(1)

    in_first = jnp.where(rot_col == 0.0, 1.0, 0.0)
    usable = jnp.where((iota((ROWS, 1), 0) % BLK).astype(F32) < cnt_col, 1.0, 0.0)
    lane = iota((ROWS, 128), 1)
    meta = jnp.where(lane == 0, in_first, 0.0)
    meta = jnp.where(lane == 1, 1.0 - in_first, meta)
    meta = jnp.where(lane == 2, in_first * usable, meta)
    meta = jnp.where(lane == 3, (1.0 - in_first) * usable, meta)
    meta_slots = dot(pack, meta.astype(BF16)).reshape(WIDE, SLOT, 128).astype(BF16)
    meta_s[...] = meta_slots
    meta_r[0] = meta_slots[0]

    def move(src, dest, k, send_sem, recv_sem, to):
        return pltpu.make_async_remote_copy(
            src_ref=src.at[k],
            dst_ref=dest.at[k],
            send_sem=send_sem,
            recv_sem=recv_sem,
            device_id=(to, z),
            device_id_type=MESH,
        )

    def send_meta(k, g, dy, i):
        move(meta_s, meta_r, k, meta_send, meta_recv, peer(dy, i)).start()

    each_slot(send_meta)

    loads[4].wait()
    qkv1[...] = dot(normed_one, w1[...]).astype(BF16)
    ring(2)
    bias = jnp.where(to_lanes(usable) > 0.0, 0.0, NEGATIVE)
    ring(3)
    for ball in range(2):
        hop(0, 2, 1 - ball).wait_recv() if ball == 0 else hop(1, 2, 1 - ball).wait_recv()
    hop(0, 3, 0).wait_recv()
    hop(1, 3, 1).wait_recv()

    attended = []
    for ball in range(2):
        pooled_all = ag[:, ball].reshape(NZ * BLOCKS // 2, WIDTH)
        pooled_kv = dot(pooled_all, w1[:, WIDTH:]).astype(BF16)
        mine = pl.ds(ball * SHARE, SHARE)
        bias_ball = jnp.concatenate(
            [bias[:, ball * SHARE : (ball + 1) * SHARE], jnp.zeros((1, NZ * BLOCKS // 2), F32)], axis=1
        )
        parts = []
        for pair in range(PAIRS):
            at = pair * 128
            query = two_heads(qkv1[mine, at : at + 128] * 0.125)
            key = jnp.concatenate(
                [qkv1[mine, WIDTH + at : WIDTH + at + 128], pooled_kv[:, at : at + 128]], axis=0
            )
            value = jnp.concatenate(
                [
                    qkv1[mine, 2 * WIDTH + at : 2 * WIDTH + at + 128],
                    pooled_kv[:, WIDTH + at : WIDTH + at + 128],
                ],
                axis=0,
            )
            parts.append(softmax_values(dot_t(query, key) + bias_ball, value).astype(BF16))
        attended.append(jnp.concatenate(parts, axis=1))
    attended_one = jnp.concatenate(attended, axis=0)
    loads[5].wait()
    layer_one = (pts[...].astype(F32) + dot(attended_one, o1[...])).astype(BF16)
    pts[...] = layer_one
    normed_two = rms_round(layer_one.astype(F32))
    slots = dot(pack, normed_two).reshape(WIDE, SLOT, WIDTH).astype(BF16)
    snd[...] = slots
    rcv[0] = slots[0]

    def send_rows(k, g, dy, i):
        move(snd, rcv, k, fwd_send, fwd_recv.at[g], peer(dy, i)).start()

    each_slot(send_rows)

    def arrived(src, dest, first, count, send_sem, recv_sem):
        return pltpu.make_async_remote_copy(
            src_ref=src.at[pl.ds(first, count)],
            dst_ref=dest.at[pl.ds(first, count)],
            send_sem=send_sem,
            recv_sem=recv_sem,
            device_id=(peer(0, 1), z),
            device_id_type=MESH,
        )

    def group(g):
        return (1, GSLOTS - 1) if g == 0 else (g * GSLOTS, GSLOTS)

    arrived(meta_s, meta_r, 1, WIDE - 1, meta_send, meta_recv).wait_recv()
    marks = meta_r[...].astype(F32).reshape(SLOTROWS, 128)
    lanes = iota((SLOTROWS, 128), 1)
    use = (lanes == 2) | (lanes == 3)
    query_mark = jnp.where(use, pltpu.roll(marks, 2, 1), 0.0).astype(BF16)
    key_mark = jnp.where(use, (1.0 - marks) * NEGATIVE, 0.0).astype(BF16)

    loads[6].wait()
    for g in range(GROUPS):
        first, count = group(g)
        arrived(snd, rcv, first, count, fwd_send, fwd_recv.at[g]).wait_recv()
        rows = rcv[g * GSLOTS : (g + 1) * GSLOTS].astype(F32).reshape(GROWS, WIDTH).astype(BF16)
        qkv2[g * GROWS : (g + 1) * GROWS, :] = dot(rows, w2[...]).astype(BF16)

    for g in range(GROUPS):
        mine = slice(g * GROWS, (g + 1) * GROWS)
        mark = query_mark[mine]
        parts = []
        for pair in range(PAIRS):
            at = pair * 128
            query = two_heads(qkv2[mine, at : at + 128] * 0.125)
            query = jnp.concatenate([query, jnp.concatenate([mark, mark], axis=0)], axis=1)
            key = jnp.concatenate([qkv2[:, WIDTH + at : WIDTH + at + 128], key_mark], axis=1)
            value = qkv2[:, 2 * WIDTH + at : 2 * WIDTH + at + 128]
            parts.append(softmax_values(dot_t(query, key), value))
        mixture = jnp.concatenate(parts, axis=1).reshape(GSLOTS, SLOT, WIDTH).astype(BF16)
        bsnd[g * GSLOTS : (g + 1) * GSLOTS] = mixture
        if g == 0:
            brcv[0] = mixture[0]

        def send_back(k, g, dy, i):
            move(bsnd, brcv, k, back_send, back_recv.at[g], source(dy, i)).start()

        each_slot(send_back, (g,))

    loads[7].wait()
    total = jnp.zeros((ROWS, WIDTH), F32)
    for g in range(GROUPS):
        first, count = group(g)
        arrived(bsnd, brcv, first, count, back_send, back_recv.at[g]).wait_recv()
        rows = brcv[g * GSLOTS : (g + 1) * GSLOTS].astype(F32).reshape(GROWS, WIDTH).astype(BF16)
        total = total + dot(unpack[:, g * GROWS : (g + 1) * GROWS], rows)
    out_ref[...] = (pts[...].astype(F32) + dot(total.astype(BF16), o2[...])).astype(BF16)

    for copy in sent:
        copy.wait_send()
    arrived(meta_s, meta_r, 1, WIDE - 1, meta_send, meta_recv).wait_send()
    arrived(snd, rcv, 1, WIDE - 1, fwd_send, fwd_recv.at[0]).wait_send()
    arrived(bsnd, brcv, 1, WIDE - 1, back_send, back_recv.at[0]).wait_send()


def on_device(points, counts, destination, rotated_ball, qkv_first, out_first, qkv_second, out_second):
    rows = points.reshape(ROWS, WIDTH)
    dma = pltpu.SemaphoreType.DMA
    hbm = pl.BlockSpec(memory_space=pltpu.MemorySpace.HBM)
    result = pl.pallas_call(
        kernel,
        out_shape=jax.ShapeDtypeStruct((ROWS, WIDTH), BF16),
        in_specs=[hbm] * 8,
        out_specs=pl.BlockSpec(memory_space=pltpu.VMEM),
        scratch_shapes=[
            pltpu.VMEM((ROWS, WIDTH), BF16),
            pltpu.VMEM((2, 32), jnp.int32),
            pltpu.VMEM((2, 32), jnp.int32),
            pltpu.VMEM((2, 32), jnp.int32),
            pltpu.VMEM((WIDTH, 3 * WIDTH), BF16),
            pltpu.VMEM((WIDTH, WIDTH), BF16),
            pltpu.VMEM((WIDTH, 3 * WIDTH), BF16),
            pltpu.VMEM((WIDTH, WIDTH), BF16),
            pltpu.VMEM((NZ, 2, BLOCKS // 2, WIDTH), BF16),
            pltpu.VMEM((WIDE, SLOT, 128), BF16),
            pltpu.VMEM((WIDE, SLOT, 128), BF16),
            pltpu.VMEM((WIDE, SLOT, WIDTH), BF16),
            pltpu.VMEM((WIDE, SLOT, WIDTH), BF16),
            pltpu.VMEM((WIDE, SLOT, WIDTH), BF16),
            pltpu.VMEM((WIDE, SLOT, WIDTH), BF16),
            pltpu.VMEM((ROWS, 3 * WIDTH), BF16),
            pltpu.VMEM((SLOTROWS, 3 * WIDTH), BF16),
            pltpu.VMEM((ROWS, SLOTROWS), BF16),
            dma((8,)),
            dma((2, 4, 2)),
            dma((NZ, 2)),
            dma,
            dma,
            dma,
            dma((GROUPS,)),
            dma,
            dma((GROUPS,)),
        ],
        compiler_params=pltpu.CompilerParams(
            collective_id=0, has_side_effects=True, vmem_limit_bytes=64 * 1024 * 1024
        ),
    )(rows, counts, destination, rotated_ball, qkv_first, out_first, qkv_second, out_second)
    return result.reshape(points.shape)


def solution(mesh):
    in_specs = (
        P("wide", "narrow", None),
        P("wide", "narrow"),
        P("wide", "narrow"),
        P("wide", "narrow"),
        P(),
        P(),
        P(),
        P(),
    )
    out_specs = P("wide", "narrow", None)
    return jax.shard_map(
        on_device, mesh=mesh, in_specs=in_specs, out_specs=out_specs, check_vma=False
    )
```

```python
import functools
import math

import jax
import jax.numpy as jnp
from jax import lax
from jax.experimental import pallas as pl
from jax.experimental.pallas import tpu as pltpu
from jax.sharding import PartitionSpec as P

HEADS = 8
BLK = 4
NX, NY, NZ = 4, 8, 8
WIDE = 2 * NX * NY
ROWS = 256
BLOCKS = 64
SHARE = 128
WIDTH = 512
SLOT = 2 * BLK
SLOTROWS = WIDE * SLOT
PAIRS = HEADS // 2
DY = (0, 4, 1, 7, 2, 6, 3, 5)
GROUPS = 4
GSLOTS = WIDE // GROUPS
GROWS = GSLOTS * SLOT

EPSILON = 1e-06
NEGATIVE = -1e30
MESH = pl.DeviceIdType.MESH
F32 = jnp.float32
BF16 = jnp.bfloat16


def iota(shape, axis):
    return lax.broadcasted_iota(jnp.int32, shape, axis)


def rms_round(values):
    scaled = values * lax.rsqrt(jnp.mean(values * values, axis=-1, keepdims=True) + EPSILON)
    return scaled.astype(BF16)


def dot(left, right):
    return jnp.dot(left, right, preferred_element_type=F32)


def dot_t(left, right):
    return lax.dot_general(left, right, (((1,), (1,)), ((), ())), preferred_element_type=F32)


def column(ref, rows, per):
    values = ref[...].astype(F32)
    half = values.shape[1]
    block = iota((rows, half), 0) // per
    lane = iota((rows, half), 1)
    first = jnp.where(block == lane, values[0:1, :], 0.0)
    second = jnp.where(block == lane + half, values[1:2, :], 0.0)
    return jnp.sum(first + second, axis=1, keepdims=True)


def to_lanes(col):
    rows = col.shape[0]
    eye = iota((rows, rows), 0) == iota((rows, rows), 1)
    return jnp.sum(jnp.where(eye, col, 0.0), axis=0, keepdims=True)


def two_heads(pair):
    low = iota(pair.shape, 1) < 64
    zero = jnp.zeros_like(pair)
    return jnp.concatenate([jnp.where(low, pair, zero), jnp.where(low, zero, pair)], axis=0)


def with_ones(values):
    return jnp.concatenate([values, jnp.ones((values.shape[0], 128), BF16)], axis=1)


def both_heads(mixed):
    mixed = mixed[:, :128] / mixed[:, 128:]
    half = mixed.shape[0] // 2
    low = iota((half, 128), 1) < 64
    return jnp.where(low, mixed[:half], mixed[half:])


def softmax_part(scores, values):
    highest = jnp.max(scores, axis=1, keepdims=True)
    weights = jnp.exp(scores - highest).astype(BF16)
    return highest, dot(weights, with_ones(values))


def softmax_rest(part, scores, values):
    before, mixed = part
    highest = jnp.maximum(before, jnp.max(scores, axis=1, keepdims=True))
    weights = jnp.exp(scores - highest).astype(BF16)
    return both_heads(mixed * jnp.exp(before - highest) + dot(weights, with_ones(values)))


def kernel(
    pts_h, cnt_h, dst_h, rot_h, w1_h, o1_h, w2_h, o2_h,
    out_ref,
    pts, cnt, dst, rot, w1, o1, w2, o2,
    ag, meta_s, meta_r, snd, rcv, bsnd, brcv, qkv1, qkv2, unpack,
    load_sem, ring_send, ring_recv, meta_send, meta_recv, fwd_send, fwd_recv, back_send, back_recv,
):
    wide = lax.axis_index("wide")
    z = lax.axis_index("narrow")
    x_me = wide // (2 * NY)
    y_me = (wide // 2) % NY
    c_me = wide % 2

    pairs = [(cnt_h, cnt), (dst_h, dst), (rot_h, rot), (w1_h, w1), (o1_h, o1), (w2_h, w2), (o2_h, o2)]
    pairs += [(pts_h.at[pl.ds(b * SHARE, SHARE)], pts.at[pl.ds(b * SHARE, SHARE)]) for b in range(2)]
    loads = [pltpu.make_async_copy(src, dest, load_sem.at[i]) for i, (src, dest) in enumerate(pairs)]
    for i in (7, 0, 8, 1, 2, 3):
        loads[i].start()

    def peer(dy, i):
        return ((x_me + i // 2) % NX) * (2 * NY) + ((y_me + dy) % NY) * 2 + (c_me + i) % 2

    def source(dy, i):
        return ((x_me + NX - i // 2) % NX) * (2 * NY) + ((y_me + NY - dy) % NY) * 2 + (c_me + i) % 2

    def each_slot(visit, groups=range(GROUPS)):
        for g in groups:
            for h in range(2):
                j = 2 * g + h

                for i in range(1 if j == 0 else 0, 8):
                    visit(8 * j + i, g, DY[j], i)

    barrier = pltpu.get_barrier_semaphore()
    for away in (1, 7, 2, 6):
        pl.semaphore_signal(barrier, inc=1, device_id=(wide, (z + away) % NZ), device_id_type=MESH)

    def greet(k, g, dy, i):
        pl.semaphore_signal(barrier, inc=1, device_id=(peer(dy, i), z), device_id_type=MESH)

    each_slot(greet)

    def hop(here, away, ball):
        there = (here + away) % NZ
        return pltpu.make_async_remote_copy(
            src_ref=ag.at[here, ball],
            dst_ref=ag.at[there, ball],
            send_sem=ring_send.at[there, ball],
            recv_sem=ring_recv.at[there, ball],
            device_id=(wide, (z + away) % NZ),
            device_id_type=MESH,
        )

    def start(here, away, ball):
        copy = hop(here, away, ball)
        copy.start()
        sent.append(copy)

    sent = []
    half = BLOCKS // 2
    loads[0].wait()
    cnt64 = column(cnt, BLOCKS, 1)
    r_b, r_l = iota((half, SHARE), 0), iota((half, SHARE), 1)
    normed = []
    for ball in range(2):
        count = cnt64[ball * half : (ball + 1) * half]
        pool = (r_l // BLK == r_b) & ((r_l % BLK).astype(F32) < count)
        pool = jnp.where(pool, 1.0, 0.0).astype(BF16)
        loads[7 + ball].wait()
        normed.append(rms_round(pts[ball * SHARE : (ball + 1) * SHARE, :].astype(F32)))
        ag[0, ball] = (dot(pool, normed[ball]) / count).astype(BF16)
        if ball == 0:
            pl.semaphore_wait(barrier, WIDE - 1 + 4)
        start(0, 2, ball)
        start(0, 6, ball)
    for ball in range(2):
        start(0, 1, ball)
        start(0, 7, ball)
    for i in (4, 5, 6):
        loads[i].start()
    normed_one = jnp.concatenate(normed, axis=0)

    loads[1].wait()
    loads[2].wait()
    cnt_col = column(cnt, ROWS, BLK)
    rot_col = column(rot, ROWS, BLK)
    dst_col = column(dst, ROWS, BLK)
    q_r, q_l = iota((ROWS, ROWS), 0), iota((ROWS, ROWS), 1)
    same = (dst_col == to_lanes(dst_col)) & (q_l // BLK < q_r // BLK)
    rank = jnp.sum(jnp.where(same, 1.0 / BLK, 0.0), axis=1, keepdims=True)
    dst_i = dst_col.astype(jnp.int32)
    d_x = ((dst_i // (2 * NY)) + NX - x_me) % NX
    d_y = ((dst_i // 2) % NY + NY - y_me) % NY
    d_c = (dst_i + c_me) % 2
    turn = jnp.where(d_y < 4, 2 * d_y, (17 - 2 * d_y) % 8)
    slot = (8 * turn + 2 * d_x + d_c) * SLOT + iota((ROWS, 1), 0) % BLK
    slot_col = slot.astype(F32) + rank * BLK
    slot_lane = to_lanes(slot_col)
    unpack[...] = jnp.where(iota((ROWS, SLOTROWS), 1).astype(F32) == slot_col, 1.0, 0.0).astype(BF16)
    pack = jnp.where(iota((SLOTROWS, ROWS), 0).astype(F32) == slot_lane, 1.0, 0.0).astype(BF16)

    in_first = jnp.where(rot_col == 0.0, 1.0, 0.0)
    usable = jnp.where((iota((ROWS, 1), 0) % BLK).astype(F32) < cnt_col, 1.0, 0.0)
    lane = iota((ROWS, 128), 1)
    meta = jnp.where(lane == 0, in_first, 0.0)
    meta = jnp.where(lane == 1, 1.0 - in_first, meta)
    meta = jnp.where(lane == 2, in_first * usable, meta)
    meta = jnp.where(lane == 3, (1.0 - in_first) * usable, meta)
    meta_slots = dot(pack, meta.astype(BF16)).reshape(WIDE, SLOT, 128).astype(BF16)
    meta_s[...] = meta_slots
    meta_r[0] = meta_slots[0]

    def move(src, dest, k, send_sem, recv_sem, to):
        return pltpu.make_async_remote_copy(
            src_ref=src.at[k],
            dst_ref=dest.at[k],
            send_sem=send_sem,
            recv_sem=recv_sem,
            device_id=(to, z),
            device_id_type=MESH,
        )

    def send_meta(k, g, dy, i):
        move(meta_s, meta_r, k, meta_send, meta_recv, peer(dy, i)).start()

    bias = jnp.where(to_lanes(usable) > 0.0, 0.0, NEGATIVE)
    loads[3].wait()
    qkv1[...] = dot(normed_one, w1[...]).astype(BF16)

    for ball in range(2):
        hop(0, 2, ball).wait_recv()
        start(2, 1, ball)
        if ball == 0:
            start(2, 2, ball)
        hop(0, 6, ball).wait_recv()
        start(6, 7, ball)
        if ball == 1:
            start(6, 6, ball)

    each_slot(send_meta)

    for ball in range(2):
        hop(0, 1, ball).wait_recv()
        hop(0, 7, ball).wait_recv()
    near = [ag[d, ball] for ball in range(2) for d in (0, 1, 2, 7)]
    near_kv = dot(jnp.concatenate(near, axis=0), w1[:, WIDTH:]).astype(BF16)
    queries, begun = [], []
    for ball in range(2):
        mine = pl.ds(ball * SHARE, SHARE)
        rows = slice(ball * 4 * half, (ball + 1) * 4 * half)
        bias_ball = jnp.concatenate(
            [bias[:, ball * SHARE : (ball + 1) * SHARE], jnp.zeros((1, 4 * half), F32)], axis=1
        )
        for pair in range(PAIRS):
            at = pair * 128
            query = two_heads(qkv1[mine, at : at + 128] * 0.125)
            key = jnp.concatenate(
                [qkv1[mine, WIDTH + at : WIDTH + at + 128], near_kv[rows, at : at + 128]], axis=0
            )
            value = jnp.concatenate(
                [
                    qkv1[mine, 2 * WIDTH + at : 2 * WIDTH + at + 128],
                    near_kv[rows, WIDTH + at : WIDTH + at + 128],
                ],
                axis=0,
            )
            queries.append(query)
            begun.append(softmax_part(dot_t(query, key) + bias_ball, value))
    for ball in range(2):
        hop(2, 1, ball).wait_recv()
        hop(6, 7, ball).wait_recv()
    hop(2, 2, 0).wait_recv()
    hop(6, 6, 1).wait_recv()
    far = [ag[d, ball] for ball in range(2) for d in (3, 4, 5, 6)]
    far_kv = dot(jnp.concatenate(far, axis=0), w1[:, WIDTH:]).astype(BF16)
    attended = []
    for ball in range(2):
        rows = slice(ball * 4 * half, (ball + 1) * 4 * half)
        parts = []
        for pair in range(PAIRS):
            at = pair * 128
            key, value = far_kv[rows, at : at + 128], far_kv[rows, WIDTH + at : WIDTH + at + 128]
            scores = dot_t(queries[ball * PAIRS + pair], key)
            parts.append(softmax_rest(begun[ball * PAIRS + pair], scores, value).astype(BF16))
        attended.append(jnp.concatenate(parts, axis=1))
    attended_one = jnp.concatenate(attended, axis=0)
    loads[4].wait()
    layer_one = (pts[...].astype(F32) + dot(attended_one, o1[...])).astype(BF16)
    pts[...] = layer_one
    normed_two = rms_round(layer_one.astype(F32))
    slots = dot(pack, normed_two).reshape(WIDE, SLOT, WIDTH).astype(BF16)
    snd[...] = slots
    rcv[0] = slots[0]

    def send_rows(k, g, dy, i):
        move(snd, rcv, k, fwd_send, fwd_recv.at[g], peer(dy, i)).start()

    each_slot(send_rows)

    def arrived(src, dest, first, count, send_sem, recv_sem):
        return pltpu.make_async_remote_copy(
            src_ref=src.at[pl.ds(first, count)],
            dst_ref=dest.at[pl.ds(first, count)],
            send_sem=send_sem,
            recv_sem=recv_sem,
            device_id=(peer(0, 1), z),
            device_id_type=MESH,
        )

    def group(g):
        return (1, GSLOTS - 1) if g == 0 else (g * GSLOTS, GSLOTS)

    arrived(meta_s, meta_r, 1, WIDE - 1, meta_send, meta_recv).wait_recv()
    marks = meta_r[...].astype(F32).reshape(SLOTROWS, 128)
    lanes = iota((SLOTROWS, 128), 1)
    use = (lanes == 2) | (lanes == 3)
    query_mark = jnp.where(use, pltpu.roll(marks, 2, 1), 0.0).astype(BF16)
    key_mark = jnp.where(use, (1.0 - marks) * NEGATIVE, 0.0).astype(BF16)

    loads[5].wait()
    for g in range(GROUPS):
        first, count = group(g)
        arrived(snd, rcv, first, count, fwd_send, fwd_recv.at[g]).wait_recv()
        rows = rcv[g * GSLOTS : (g + 1) * GSLOTS].astype(F32).reshape(GROWS, WIDTH).astype(BF16)
        qkv2[g * GROWS : (g + 1) * GROWS, :] = dot(rows, w2[...]).astype(BF16)

    for g in range(GROUPS):
        mine = slice(g * GROWS, (g + 1) * GROWS)
        mark = query_mark[mine]
        parts = []
        for pair in range(PAIRS):
            at = pair * 128
            query = two_heads(qkv2[mine, at : at + 128] * 0.125)
            query = jnp.concatenate([query, jnp.concatenate([mark, mark], axis=0)], axis=1)
            key = jnp.concatenate([qkv2[:, WIDTH + at : WIDTH + at + 128], key_mark], axis=1)
            value = qkv2[:, 2 * WIDTH + at : 2 * WIDTH + at + 128]
            parts.append(both_heads(softmax_part(dot_t(query, key), value)[1]))
        mixture = jnp.concatenate(parts, axis=1).reshape(GSLOTS, SLOT, WIDTH).astype(BF16)
        bsnd[g * GSLOTS : (g + 1) * GSLOTS] = mixture
        if g == 0:
            brcv[0] = mixture[0]

        def send_back(k, g, dy, i):
            move(bsnd, brcv, k, back_send, back_recv.at[g], source(dy, i)).start()

        each_slot(send_back, (g,))

    loads[6].wait()
    total = jnp.zeros((ROWS, WIDTH), F32)
    for g in range(GROUPS):
        first, count = group(g)
        arrived(bsnd, brcv, first, count, back_send, back_recv.at[g]).wait_recv()
        rows = brcv[g * GSLOTS : (g + 1) * GSLOTS].astype(F32).reshape(GROWS, WIDTH).astype(BF16)
        total = total + dot(unpack[:, g * GROWS : (g + 1) * GROWS], rows)
    out_ref[...] = (pts[...].astype(F32) + dot(total.astype(BF16), o2[...])).astype(BF16)

    for copy in sent:
        copy.wait_send()
    arrived(meta_s, meta_r, 1, WIDE - 1, meta_send, meta_recv).wait_send()
    arrived(snd, rcv, 1, WIDE - 1, fwd_send, fwd_recv.at[0]).wait_send()
    arrived(bsnd, brcv, 1, WIDE - 1, back_send, back_recv.at[0]).wait_send()


def on_device(points, counts, destination, rotated_ball, qkv_first, out_first, qkv_second, out_second):
    rows = points.reshape(ROWS, WIDTH)
    dma = pltpu.SemaphoreType.DMA
    hbm = pl.BlockSpec(memory_space=pltpu.MemorySpace.HBM)
    result = pl.pallas_call(
        kernel,
        out_shape=jax.ShapeDtypeStruct((ROWS, WIDTH), BF16),
        in_specs=[hbm] * 8,
        out_specs=pl.BlockSpec(memory_space=pltpu.VMEM),
        scratch_shapes=[
            pltpu.VMEM((ROWS, WIDTH), BF16),
            pltpu.VMEM((2, 32), jnp.int32),
            pltpu.VMEM((2, 32), jnp.int32),
            pltpu.VMEM((2, 32), jnp.int32),
            pltpu.VMEM((WIDTH, 3 * WIDTH), BF16),
            pltpu.VMEM((WIDTH, WIDTH), BF16),
            pltpu.VMEM((WIDTH, 3 * WIDTH), BF16),
            pltpu.VMEM((WIDTH, WIDTH), BF16),
            pltpu.VMEM((NZ, 2, BLOCKS // 2, WIDTH), BF16),
            pltpu.VMEM((WIDE, SLOT, 128), BF16),
            pltpu.VMEM((WIDE, SLOT, 128), BF16),
            pltpu.VMEM((WIDE, SLOT, WIDTH), BF16),
            pltpu.VMEM((WIDE, SLOT, WIDTH), BF16),
            pltpu.VMEM((WIDE, SLOT, WIDTH), BF16),
            pltpu.VMEM((WIDE, SLOT, WIDTH), BF16),
            pltpu.VMEM((ROWS, 3 * WIDTH), BF16),
            pltpu.VMEM((SLOTROWS, 3 * WIDTH), BF16),
            pltpu.VMEM((ROWS, SLOTROWS), BF16),
            dma((9,)),
            dma((NZ, 2)),
            dma((NZ, 2)),
            dma,
            dma,
            dma,
            dma((GROUPS,)),
            dma,
            dma((GROUPS,)),
        ],
        compiler_params=pltpu.CompilerParams(
            collective_id=0, has_side_effects=True, vmem_limit_bytes=48 * 1024 * 1024
        ),
    )(*[pltpu.with_memory_space_constraint(a, pltpu.HBM) for a in (rows, counts, destination, rotated_ball, qkv_first, out_first, qkv_second, out_second)])
    return result.reshape(points.shape)


def solution(mesh):
    in_specs = (
        P("wide", "narrow", None),
        P("wide", "narrow"),
        P("wide", "narrow"),
        P("wide", "narrow"),
        P(),
        P(),
        P(),
        P(),
    )
    out_specs = P("wide", "narrow", None)
    return jax.shard_map(
        on_device, mesh=mesh, in_specs=in_specs, out_specs=out_specs, check_vma=False
    )
```

```python
import functools
import math

import jax
import jax.numpy as jnp
from jax import lax
from jax.experimental import pallas as pl
from jax.experimental.pallas import tpu as pltpu
from jax.sharding import PartitionSpec as P

HEADS = 8
BLK = 4
NX, NY, NZ = 4, 8, 8
WIDE = 2 * NX * NY
ROWS = 256
BLOCKS = 64
SHARE = 128
WIDTH = 512
SLOT = 2 * BLK
SLOTROWS = WIDE * SLOT
PAIRS = HEADS // 2
DY = (0, 4, 1, 7, 2, 6, 3, 5)
GROUPS = 4
GSLOTS = WIDE // GROUPS
GROWS = GSLOTS * SLOT

EPSILON = 1e-06
NEGATIVE = -1e30
MESH = pl.DeviceIdType.MESH
F32 = jnp.float32
BF16 = jnp.bfloat16


def iota(shape, axis):
    return lax.broadcasted_iota(jnp.int32, shape, axis)


def rms_round(values):
    scaled = values * lax.rsqrt(jnp.mean(values * values, axis=-1, keepdims=True) + EPSILON)
    return scaled.astype(BF16)


def dot(left, right):
    return jnp.dot(left, right, preferred_element_type=F32)


def dot_t(left, right):
    return lax.dot_general(left, right, (((1,), (1,)), ((), ())), preferred_element_type=F32)


def column(ref, rows, per):
    values = ref[...].astype(F32)
    half = values.shape[1]
    block = iota((rows, half), 0) // per
    lane = iota((rows, half), 1)
    first = jnp.where(block == lane, values[0:1, :], 0.0)
    second = jnp.where(block == lane + half, values[1:2, :], 0.0)
    return jnp.sum(first + second, axis=1, keepdims=True)


def to_lanes(col):
    rows = col.shape[0]
    eye = iota((rows, rows), 0) == iota((rows, rows), 1)
    return jnp.sum(jnp.where(eye, col, 0.0), axis=0, keepdims=True)


def two_heads(pair):
    low = iota(pair.shape, 1) < 64
    zero = jnp.zeros_like(pair)
    return jnp.concatenate([jnp.where(low, pair, zero), jnp.where(low, zero, pair)], axis=0)


def with_ones(values):
    return jnp.concatenate([values, jnp.ones((values.shape[0], 128), BF16)], axis=1)


def both_heads(mixed):
    mixed = mixed[:, :128] / mixed[:, 128:]
    half = mixed.shape[0] // 2
    low = iota((half, 128), 1) < 64
    return jnp.where(low, mixed[:half], mixed[half:])


def softmax_part(scores, values):
    highest = jnp.max(scores, axis=1, keepdims=True)
    weights = jnp.exp(scores - highest).astype(BF16)
    return highest, dot(weights, with_ones(values))


def softmax_rest(part, scores, values):
    before, mixed = part
    highest = jnp.maximum(before, jnp.max(scores, axis=1, keepdims=True))
    weights = jnp.exp(scores - highest).astype(BF16)
    return both_heads(mixed * jnp.exp(before - highest) + dot(weights, with_ones(values)))


def kernel(
    pts_h, cnt_h, dst_h, rot_h, w1_h, o1_h, w2_h, o2_h,
    out_ref,
    pts, cnt, dst, rot, w1, o1, w2, o2,
    ag, meta_s, meta_r, snd, rcv, bsnd, brcv, qkv1, qkv2, unpack,
    load_sem, ring_send, ring_recv, meta_send, meta_recv, fwd_send, fwd_recv, back_send, back_recv,
):
    wide = lax.axis_index("wide")
    z = lax.axis_index("narrow")
    x_me = wide // (2 * NY)
    y_me = (wide // 2) % NY
    c_me = wide % 2

    pairs = [(cnt_h, cnt), (dst_h, dst), (rot_h, rot), (w1_h, w1), (o1_h, o1), (w2_h, w2), (o2_h, o2)]
    pairs += [(pts_h.at[pl.ds(b * SHARE, SHARE)], pts.at[pl.ds(b * SHARE, SHARE)]) for b in range(2)]
    loads = [pltpu.make_async_copy(src, dest, load_sem.at[i]) for i, (src, dest) in enumerate(pairs)]
    for i in (7, 0, 8, 1, 2, 3):
        loads[i].start()

    def peer(dy, i):
        return ((x_me + i // 2) % NX) * (2 * NY) + ((y_me + dy) % NY) * 2 + (c_me + i) % 2

    def source(dy, i):
        return ((x_me + NX - i // 2) % NX) * (2 * NY) + ((y_me + NY - dy) % NY) * 2 + (c_me + i) % 2

    def each_slot(visit, groups=range(GROUPS), order=None):
        for j, i in order or [(j, i) for j in range(8) for i in range(8)]:
            if (j, i) != (0, 0) and j // 2 in groups:
                visit(8 * j + i, j // 2, DY[j], i)

    barrier = pltpu.get_barrier_semaphore()
    for away in (1, 7, 2, 6):
        pl.semaphore_signal(barrier, inc=1, device_id=(wide, (z + away) % NZ), device_id_type=MESH)

    def greet(k, g, dy, i):
        pl.semaphore_signal(barrier, inc=1, device_id=(peer(dy, i), z), device_id_type=MESH)

    each_slot(greet)

    def hop(here, away, ball):
        there = (here + away) % NZ
        return pltpu.make_async_remote_copy(
            src_ref=ag.at[here, ball],
            dst_ref=ag.at[there, ball],
            send_sem=ring_send.at[there, ball],
            recv_sem=ring_recv.at[there, ball],
            device_id=(wide, (z + away) % NZ),
            device_id_type=MESH,
        )

    def start(here, away, ball):
        copy = hop(here, away, ball)
        copy.start()
        sent.append(copy)

    sent = []
    half = BLOCKS // 2
    loads[0].wait()
    cnt64 = column(cnt, BLOCKS, 1)
    r_b, r_l = iota((half, SHARE), 0), iota((half, SHARE), 1)
    normed = []
    for ball in range(2):
        count = cnt64[ball * half : (ball + 1) * half]
        pool = (r_l // BLK == r_b) & ((r_l % BLK).astype(F32) < count)
        pool = jnp.where(pool, 1.0, 0.0).astype(BF16)
        loads[7 + ball].wait()
        normed.append(rms_round(pts[ball * SHARE : (ball + 1) * SHARE, :].astype(F32)))
        ag[0, ball] = (dot(pool, normed[ball]) / count).astype(BF16)
        if ball == 0:
            pl.semaphore_wait(barrier, WIDE - 1 + 4)
        start(0, 2, ball)
        start(0, 6, ball)
    for ball in range(2):
        start(0, 1, ball)
        start(0, 7, ball)
    for i in (4, 5, 6):
        loads[i].start()
    normed_one = jnp.concatenate(normed, axis=0)

    loads[1].wait()
    loads[2].wait()
    cnt_col = column(cnt, ROWS, BLK)
    rot_col = column(rot, ROWS, BLK)
    dst_col = column(dst, ROWS, BLK)
    q_r, q_l = iota((ROWS, ROWS), 0), iota((ROWS, ROWS), 1)
    same = (dst_col == to_lanes(dst_col)) & (q_l // BLK < q_r // BLK)
    rank = jnp.sum(jnp.where(same, 1.0 / BLK, 0.0), axis=1, keepdims=True)
    dst_i = dst_col.astype(jnp.int32)
    d_x = ((dst_i // (2 * NY)) + NX - x_me) % NX
    d_y = ((dst_i // 2) % NY + NY - y_me) % NY
    d_c = (dst_i + c_me) % 2
    turn = jnp.where(d_y < 4, 2 * d_y, (17 - 2 * d_y) % 8)
    slot = (8 * turn + 2 * d_x + d_c) * SLOT + iota((ROWS, 1), 0) % BLK
    slot_col = slot.astype(F32) + rank * BLK
    slot_lane = to_lanes(slot_col)
    unpack[...] = jnp.where(iota((ROWS, SLOTROWS), 1).astype(F32) == slot_col, 1.0, 0.0).astype(BF16)
    pack = jnp.where(iota((SLOTROWS, ROWS), 0).astype(F32) == slot_lane, 1.0, 0.0).astype(BF16)

    in_first = jnp.where(rot_col == 0.0, 1.0, 0.0)
    usable = jnp.where((iota((ROWS, 1), 0) % BLK).astype(F32) < cnt_col, 1.0, 0.0)
    lane = iota((ROWS, 128), 1)
    meta = jnp.where(lane == 0, in_first, 0.0)
    meta = jnp.where(lane == 1, 1.0 - in_first, meta)
    meta = jnp.where(lane == 2, in_first * usable, meta)
    meta = jnp.where(lane == 3, (1.0 - in_first) * usable, meta)
    meta_slots = dot(pack, meta.astype(BF16)).reshape(WIDE, SLOT, 128).astype(BF16)
    meta_s[...] = meta_slots
    meta_r[0] = meta_slots[0]

    def move(src, dest, k, send_sem, recv_sem, to):
        return pltpu.make_async_remote_copy(
            src_ref=src.at[k],
            dst_ref=dest.at[k],
            send_sem=send_sem,
            recv_sem=recv_sem,
            device_id=(to, z),
            device_id_type=MESH,
        )

    def send_meta(k, g, dy, i):
        move(meta_s, meta_r, k, meta_send, meta_recv, peer(dy, i)).start()

    bias = jnp.where(to_lanes(usable) > 0.0, 0.0, NEGATIVE)
    loads[3].wait()
    qkv1[...] = dot(normed_one, w1[...]).astype(BF16)

    for ball in range(2):
        hop(0, 2, ball).wait_recv()
        start(2, 1, ball)
        if ball == 0:
            start(2, 2, ball)
        hop(0, 6, ball).wait_recv()
        start(6, 7, ball)
        if ball == 1:
            start(6, 6, ball)

    each_slot(send_meta)

    for ball in range(2):
        hop(0, 1, ball).wait_recv()
        hop(0, 7, ball).wait_recv()
    near = [ag[d, ball] for ball in range(2) for d in (0, 1, 2, 7)]
    near_kv = dot(jnp.concatenate(near, axis=0), w1[:, WIDTH:]).astype(BF16)
    queries, begun = [], []
    for ball in range(2):
        mine = pl.ds(ball * SHARE, SHARE)
        rows = slice(ball * 4 * half, (ball + 1) * 4 * half)
        bias_ball = jnp.concatenate(
            [bias[:, ball * SHARE : (ball + 1) * SHARE], jnp.zeros((1, 4 * half), F32)], axis=1
        )
        for pair in range(PAIRS):
            at = pair * 128
            query = two_heads(qkv1[mine, at : at + 128] * 0.125)
            key = jnp.concatenate(
                [qkv1[mine, WIDTH + at : WIDTH + at + 128], near_kv[rows, at : at + 128]], axis=0
            )
            value = jnp.concatenate(
                [
                    qkv1[mine, 2 * WIDTH + at : 2 * WIDTH + at + 128],
                    near_kv[rows, WIDTH + at : WIDTH + at + 128],
                ],
                axis=0,
            )
            queries.append(query)
            begun.append(softmax_part(dot_t(query, key) + bias_ball, value))
    for ball in range(2):
        hop(2, 1, ball).wait_recv()
        hop(6, 7, ball).wait_recv()
    hop(2, 2, 0).wait_recv()
    hop(6, 6, 1).wait_recv()
    far = [ag[d, ball] for ball in range(2) for d in (3, 4, 5, 6)]
    far_kv = dot(jnp.concatenate(far, axis=0), w1[:, WIDTH:]).astype(BF16)
    attended = []
    for ball in range(2):
        rows = slice(ball * 4 * half, (ball + 1) * 4 * half)
        parts = []
        for pair in range(PAIRS):
            at = pair * 128
            key, value = far_kv[rows, at : at + 128], far_kv[rows, WIDTH + at : WIDTH + at + 128]
            scores = dot_t(queries[ball * PAIRS + pair], key)
            parts.append(softmax_rest(begun[ball * PAIRS + pair], scores, value).astype(BF16))
        attended.append(jnp.concatenate(parts, axis=1))
    attended_one = jnp.concatenate(attended, axis=0)
    loads[4].wait()
    layer_one = (pts[...].astype(F32) + dot(attended_one, o1[...])).astype(BF16)
    pts[...] = layer_one
    normed_two = rms_round(layer_one.astype(F32))
    slots = dot(pack, normed_two).reshape(WIDE, SLOT, WIDTH).astype(BF16)
    snd[...] = slots
    rcv[0] = slots[0]

    def send_rows(k, g, dy, i):
        move(snd, rcv, k, fwd_send, fwd_recv.at[g], peer(dy, i)).start()

    each_slot(send_rows, order=[(j, i) for j in range(8) for i in (4, 5, 2, 6, 3, 7, 0, 1)])

    def arrived(src, dest, first, count, send_sem, recv_sem):
        return pltpu.make_async_remote_copy(
            src_ref=src.at[pl.ds(first, count)],
            dst_ref=dest.at[pl.ds(first, count)],
            send_sem=send_sem,
            recv_sem=recv_sem,
            device_id=(peer(0, 1), z),
            device_id_type=MESH,
        )

    def group(g):
        return (1, GSLOTS - 1) if g == 0 else (g * GSLOTS, GSLOTS)

    arrived(meta_s, meta_r, 1, WIDE - 1, meta_send, meta_recv).wait_recv()
    marks = meta_r[...].astype(F32).reshape(SLOTROWS, 128)
    lanes = iota((SLOTROWS, 128), 1)
    use = (lanes == 2) | (lanes == 3)
    query_mark = jnp.where(use, pltpu.roll(marks, 2, 1), 0.0).astype(BF16)
    key_mark = jnp.where(use, (1.0 - marks) * NEGATIVE, 0.0).astype(BF16)

    loads[5].wait()
    def project(g):
        first, count = group(g)
        arrived(snd, rcv, first, count, fwd_send, fwd_recv.at[g]).wait_recv()
        rows = rcv[g * GSLOTS : (g + 1) * GSLOTS].astype(F32).reshape(GROWS, WIDTH).astype(BF16)
        qkv2[g * GROWS : (g + 1) * GROWS, :] = dot(rows, w2[...]).astype(BF16)

    def scored(g, pair, keys):
        at = pair * 128
        mark = query_mark[g * GROWS : (g + 1) * GROWS]
        query = two_heads(qkv2[g * GROWS : (g + 1) * GROWS, at : at + 128] * 0.125)
        query = jnp.concatenate([query, jnp.concatenate([mark, mark], axis=0)], axis=1)
        key = jnp.concatenate([qkv2[keys, WIDTH + at : WIDTH + at + 128], key_mark[keys]], axis=1)
        return dot_t(query, key), qkv2[keys, 2 * WIDTH + at : 2 * WIDTH + at + 128]

    last = GROUPS - 1
    early, late = slice(0, last * GROWS), slice(last * GROWS, SLOTROWS)
    for g in range(last):
        project(g)
    begun_two = [[softmax_part(*scored(g, pair, early)) for pair in range(PAIRS)] for g in range(1)]
    project(last)

    for g in range(GROUPS):
        parts = []
        for pair in range(PAIRS):
            if g < 1:
                parts.append(softmax_rest(begun_two[g][pair], *scored(g, pair, late)))
            else:
                parts.append(both_heads(softmax_part(*scored(g, pair, slice(0, SLOTROWS)))[1]))
        mixture = jnp.concatenate(parts, axis=1).reshape(GSLOTS, SLOT, WIDTH).astype(BF16)
        bsnd[g * GSLOTS : (g + 1) * GSLOTS] = mixture
        if g == 0:
            brcv[0] = mixture[0]

        def send_back(k, g, dy, i):
            move(bsnd, brcv, k, back_send, back_recv.at[g], source(dy, i)).start()

        each_slot(send_back, (g,), [(j, i) for j in range(8) for i in (4, 5, 2, 6, 3, 7, 0, 1)])

    loads[6].wait()
    total = jnp.zeros((ROWS, WIDTH), F32)
    for g in range(GROUPS):
        first, count = group(g)
        arrived(bsnd, brcv, first, count, back_send, back_recv.at[g]).wait_recv()
        rows = brcv[g * GSLOTS : (g + 1) * GSLOTS].astype(F32).reshape(GROWS, WIDTH).astype(BF16)
        total = total + dot(unpack[:, g * GROWS : (g + 1) * GROWS], rows)
    out_ref[...] = (pts[...].astype(F32) + dot(total.astype(BF16), o2[...])).astype(BF16)

    for copy in sent:
        copy.wait_send()
    arrived(meta_s, meta_r, 1, WIDE - 1, meta_send, meta_recv).wait_send()
    arrived(snd, rcv, 1, WIDE - 1, fwd_send, fwd_recv.at[0]).wait_send()
    arrived(bsnd, brcv, 1, WIDE - 1, back_send, back_recv.at[0]).wait_send()


def on_device(points, counts, destination, rotated_ball, qkv_first, out_first, qkv_second, out_second):
    rows = points.reshape(ROWS, WIDTH)
    dma = pltpu.SemaphoreType.DMA
    hbm = pl.BlockSpec(memory_space=pltpu.MemorySpace.HBM)
    result = pl.pallas_call(
        kernel,
        out_shape=jax.ShapeDtypeStruct((ROWS, WIDTH), BF16),
        in_specs=[hbm] * 8,
        out_specs=pl.BlockSpec(memory_space=pltpu.VMEM),
        scratch_shapes=[
            pltpu.VMEM((ROWS, WIDTH), BF16),
            pltpu.VMEM((2, 32), jnp.int32),
            pltpu.VMEM((2, 32), jnp.int32),
            pltpu.VMEM((2, 32), jnp.int32),
            pltpu.VMEM((WIDTH, 3 * WIDTH), BF16),
            pltpu.VMEM((WIDTH, WIDTH), BF16),
            pltpu.VMEM((WIDTH, 3 * WIDTH), BF16),
            pltpu.VMEM((WIDTH, WIDTH), BF16),
            pltpu.VMEM((NZ, 2, BLOCKS // 2, WIDTH), BF16),
            pltpu.VMEM((WIDE, SLOT, 128), BF16),
            pltpu.VMEM((WIDE, SLOT, 128), BF16),
            pltpu.VMEM((WIDE, SLOT, WIDTH), BF16),
            pltpu.VMEM((WIDE, SLOT, WIDTH), BF16),
            pltpu.VMEM((WIDE, SLOT, WIDTH), BF16),
            pltpu.VMEM((WIDE, SLOT, WIDTH), BF16),
            pltpu.VMEM((ROWS, 3 * WIDTH), BF16),
            pltpu.VMEM((SLOTROWS, 3 * WIDTH), BF16),
            pltpu.VMEM((ROWS, SLOTROWS), BF16),
            dma((9,)),
            dma((NZ, 2)),
            dma((NZ, 2)),
            dma,
            dma,
            dma,
            dma((GROUPS,)),
            dma,
            dma((GROUPS,)),
        ],
        compiler_params=pltpu.CompilerParams(
            collective_id=0, has_side_effects=True, vmem_limit_bytes=48 * 1024 * 1024
        ),
    )(*[pltpu.with_memory_space_constraint(a, pltpu.HBM) for a in (rows, counts, destination, rotated_ball, qkv_first, out_first, qkv_second, out_second)])
    return result.reshape(points.shape)


def solution(mesh):
    in_specs = (
        P("wide", "narrow", None),
        P("wide", "narrow"),
        P("wide", "narrow"),
        P("wide", "narrow"),
        P(),
        P(),
        P(),
        P(),
    )
    out_specs = P("wide", "narrow", None)
    return jax.shard_map(
        on_device, mesh=mesh, in_specs=in_specs, out_specs=out_specs, check_vma=False
    )
```

```python
import functools
import math

import jax
import jax.numpy as jnp
from jax import lax
from jax.experimental import pallas as pl
from jax.experimental.pallas import tpu as pltpu
from jax.sharding import PartitionSpec as P

HEADS = 8
BLK = 4
NX, NY, NZ = 4, 8, 8
WIDE = 2 * NX * NY
ROWS = 256
BLOCKS = 64
SHARE = 128
WIDTH = 512
SLOT = 2 * BLK
SLOTROWS = WIDE * SLOT
PAIRS = HEADS // 2
DY = (0, 4, 1, 7, 2, 6, 3, 5)
GROUPS = 4
GSLOTS = WIDE // GROUPS
GROWS = GSLOTS * SLOT

EPSILON = 1e-06
NEGATIVE = -1e30
MESH = pl.DeviceIdType.MESH
F32 = jnp.float32
BF16 = jnp.bfloat16


def iota(shape, axis):
    return lax.broadcasted_iota(jnp.int32, shape, axis)


def rms_round(values):
    scaled = values * lax.rsqrt(jnp.mean(values * values, axis=-1, keepdims=True) + EPSILON)
    return scaled.astype(BF16)


def dot(left, right):
    return jnp.dot(left, right, preferred_element_type=F32)


def dot_t(left, right):
    return lax.dot_general(left, right, (((1,), (1,)), ((), ())), preferred_element_type=F32)


def column(ref, rows, per):
    values = ref[...].astype(F32)
    half = values.shape[1]
    block = iota((rows, half), 0) // per
    lane = iota((rows, half), 1)
    first = jnp.where(block == lane, values[0:1, :], 0.0)
    second = jnp.where(block == lane + half, values[1:2, :], 0.0)
    return jnp.sum(first + second, axis=1, keepdims=True)


def to_lanes(col):
    rows = col.shape[0]
    eye = iota((rows, rows), 0) == iota((rows, rows), 1)
    return jnp.sum(jnp.where(eye, col, 0.0), axis=0, keepdims=True)


def two_heads(pair):
    low = iota(pair.shape, 1) < 64
    zero = jnp.zeros_like(pair)
    return jnp.concatenate([jnp.where(low, pair, zero), jnp.where(low, zero, pair)], axis=0)


def with_ones(values):
    return jnp.concatenate([values, jnp.ones((values.shape[0], 128), BF16)], axis=1)


def both_heads(mixed):
    mixed = mixed[:, :128] / mixed[:, 128:]
    half = mixed.shape[0] // 2
    low = iota((half, 128), 1) < 64
    return jnp.where(low, mixed[:half], mixed[half:])


def softmax_part(scores, values):
    highest = jnp.max(scores, axis=1, keepdims=True)
    weights = jnp.exp(scores - highest).astype(BF16)
    return highest, dot(weights, with_ones(values))


def softmax_rest(part, scores, values):
    before, mixed = part
    highest = jnp.maximum(before, jnp.max(scores, axis=1, keepdims=True))
    weights = jnp.exp(scores - highest).astype(BF16)
    return both_heads(mixed * jnp.exp(before - highest) + dot(weights, with_ones(values)))


def kernel(
    pts_h, cnt_h, dst_h, rot_h, w1_h, o1_h, w2_h, o2_h,
    out_ref,
    pts, cnt, dst, rot, w1, o1, w2, o2,
    ag, meta_s, meta_r, snd, rcv, bsnd, brcv, qkv1, qkv2, unpack,
    load_sem, ring_send, ring_recv, meta_send, meta_recv, fwd_send, fwd_recv, back_send, back_recv,
):
    wide = lax.axis_index("wide")
    z = lax.axis_index("narrow")
    x_me = wide // (2 * NY)
    y_me = (wide // 2) % NY
    c_me = wide % 2

    pairs = [(cnt_h, cnt), (dst_h, dst), (rot_h, rot), (w1_h, w1), (o1_h, o1), (w2_h, w2), (o2_h, o2)]
    pairs += [(pts_h.at[pl.ds(b * SHARE, SHARE)], pts.at[pl.ds(b * SHARE, SHARE)]) for b in range(2)]
    loads = [pltpu.make_async_copy(src, dest, load_sem.at[i]) for i, (src, dest) in enumerate(pairs)]
    for i in (7, 0, 8, 1, 2, 3):
        loads[i].start()

    def peer(dy, i):
        return ((x_me + i // 2) % NX) * (2 * NY) + ((y_me + dy) % NY) * 2 + (c_me + i) % 2

    def source(dy, i):
        return ((x_me + NX - i // 2) % NX) * (2 * NY) + ((y_me + NY - dy) % NY) * 2 + (c_me + i) % 2

    def each_slot(visit, groups=range(GROUPS), order=None):
        for j, i in order or [(j, i) for j in range(8) for i in range(8)]:
            if (j, i) != (0, 0) and j // 2 in groups:
                visit(8 * j + i, j // 2, DY[j], i)

    barrier = pltpu.get_barrier_semaphore()
    for away in (1, 7, 2, 6):
        pl.semaphore_signal(barrier, inc=1, device_id=(wide, (z + away) % NZ), device_id_type=MESH)

    def greet(k, g, dy, i):
        pl.semaphore_signal(barrier, inc=1, device_id=(peer(dy, i), z), device_id_type=MESH)

    each_slot(greet)

    def hop(here, away, ball):
        there = (here + away) % NZ
        return pltpu.make_async_remote_copy(
            src_ref=ag.at[here, ball],
            dst_ref=ag.at[there, ball],
            send_sem=ring_send.at[there, ball],
            recv_sem=ring_recv.at[there, ball],
            device_id=(wide, (z + away) % NZ),
            device_id_type=MESH,
        )

    def start(here, away, ball):
        copy = hop(here, away, ball)
        copy.start()
        sent.append(copy)

    sent = []
    half = BLOCKS // 2
    loads[0].wait()
    cnt64 = column(cnt, BLOCKS, 1)
    r_b, r_l = iota((half, SHARE), 0), iota((half, SHARE), 1)
    normed = []
    for ball in range(2):
        count = cnt64[ball * half : (ball + 1) * half]
        pool = (r_l // BLK == r_b) & ((r_l % BLK).astype(F32) < count)
        pool = jnp.where(pool, 1.0, 0.0).astype(BF16)
        loads[7 + ball].wait()
        normed.append(rms_round(pts[ball * SHARE : (ball + 1) * SHARE, :].astype(F32)))
        ag[0, ball] = (dot(pool, normed[ball]) / count).astype(BF16)
        if ball == 0:
            pl.semaphore_wait(barrier, WIDE - 1 + 4)
        start(0, 2, ball)
        start(0, 6, ball)
    for ball in range(2):
        start(0, 1, ball)
        start(0, 7, ball)
    for i in (4, 5, 6):
        loads[i].start()
    normed_one = jnp.concatenate(normed, axis=0)

    loads[1].wait()
    loads[2].wait()
    cnt_col = column(cnt, ROWS, BLK)
    rot_col = column(rot, ROWS, BLK)
    dst_col = column(dst, ROWS, BLK)
    q_r, q_l = iota((ROWS, ROWS), 0), iota((ROWS, ROWS), 1)
    same = (dst_col == to_lanes(dst_col)) & (q_l // BLK < q_r // BLK)
    rank = jnp.sum(jnp.where(same, 1.0 / BLK, 0.0), axis=1, keepdims=True)
    dst_i = dst_col.astype(jnp.int32)
    d_x = ((dst_i // (2 * NY)) + NX - x_me) % NX
    d_y = ((dst_i // 2) % NY + NY - y_me) % NY
    d_c = (dst_i + c_me) % 2
    turn = jnp.where(d_y < 4, 2 * d_y, (17 - 2 * d_y) % 8)
    slot = (8 * turn + 2 * d_x + d_c) * SLOT + iota((ROWS, 1), 0) % BLK
    slot_col = slot.astype(F32) + rank * BLK
    slot_lane = to_lanes(slot_col)
    unpack[...] = jnp.where(iota((ROWS, SLOTROWS), 1).astype(F32) == slot_col, 1.0, 0.0).astype(BF16)
    pack = jnp.where(iota((SLOTROWS, ROWS), 0).astype(F32) == slot_lane, 1.0, 0.0).astype(BF16)

    in_first = jnp.where(rot_col == 0.0, 1.0, 0.0)
    usable = jnp.where((iota((ROWS, 1), 0) % BLK).astype(F32) < cnt_col, 1.0, 0.0)
    lane = iota((ROWS, 128), 1)
    meta = jnp.where(lane == 0, in_first, 0.0)
    meta = jnp.where(lane == 1, 1.0 - in_first, meta)
    meta = jnp.where(lane == 2, in_first * usable, meta)
    meta = jnp.where(lane == 3, (1.0 - in_first) * usable, meta)
    meta_slots = dot(pack, meta.astype(BF16)).reshape(WIDE, SLOT, 128).astype(BF16)
    meta_s[...] = meta_slots
    meta_r[0] = meta_slots[0]

    def move(src, dest, k, send_sem, recv_sem, to):
        return pltpu.make_async_remote_copy(
            src_ref=src.at[k],
            dst_ref=dest.at[k],
            send_sem=send_sem,
            recv_sem=recv_sem,
            device_id=(to, z),
            device_id_type=MESH,
        )

    def send_meta(k, g, dy, i):
        move(meta_s, meta_r, k, meta_send, meta_recv, peer(dy, i)).start()

    bias = jnp.where(to_lanes(usable) > 0.0, 0.0, NEGATIVE)
    loads[3].wait()
    qkv1[...] = dot(normed_one, w1[...]).astype(BF16)

    for ball in range(2):
        hop(0, 2, ball).wait_recv()
        start(2, 1, ball)
        if ball == 0:
            start(2, 2, ball)
        hop(0, 6, ball).wait_recv()
        start(6, 7, ball)
        if ball == 1:
            start(6, 6, ball)

    each_slot(send_meta)

    for ball in range(2):
        hop(0, 1, ball).wait_recv()
        hop(0, 7, ball).wait_recv()
    near = [ag[d, ball] for ball in range(2) for d in (0, 1, 2, 7)]
    near_kv = dot(jnp.concatenate(near, axis=0), w1[:, WIDTH:]).astype(BF16)
    queries, begun = [], []
    for ball in range(2):
        mine = pl.ds(ball * SHARE, SHARE)
        rows = slice(ball * 4 * half, (ball + 1) * 4 * half)
        bias_ball = jnp.concatenate(
            [bias[:, ball * SHARE : (ball + 1) * SHARE], jnp.zeros((1, 4 * half), F32)], axis=1
        )
        for pair in range(PAIRS):
            at = pair * 128
            query = two_heads(qkv1[mine, at : at + 128] * 0.125)
            key = jnp.concatenate(
                [qkv1[mine, WIDTH + at : WIDTH + at + 128], near_kv[rows, at : at + 128]], axis=0
            )
            value = jnp.concatenate(
                [
                    qkv1[mine, 2 * WIDTH + at : 2 * WIDTH + at + 128],
                    near_kv[rows, WIDTH + at : WIDTH + at + 128],
                ],
                axis=0,
            )
            queries.append(query)
            begun.append(softmax_part(dot_t(query, key) + bias_ball, value))
    for ball in range(2):
        hop(2, 1, ball).wait_recv()
        hop(6, 7, ball).wait_recv()
    hop(2, 2, 0).wait_recv()
    hop(6, 6, 1).wait_recv()
    far = [ag[d, ball] for ball in range(2) for d in (3, 4, 5, 6)]
    far_kv = dot(jnp.concatenate(far, axis=0), w1[:, WIDTH:]).astype(BF16)
    attended = []
    for ball in range(2):
        rows = slice(ball * 4 * half, (ball + 1) * 4 * half)
        parts = []
        for pair in range(PAIRS):
            at = pair * 128
            key, value = far_kv[rows, at : at + 128], far_kv[rows, WIDTH + at : WIDTH + at + 128]
            scores = dot_t(queries[ball * PAIRS + pair], key)
            parts.append(softmax_rest(begun[ball * PAIRS + pair], scores, value).astype(BF16))
        attended.append(jnp.concatenate(parts, axis=1))
    attended_one = jnp.concatenate(attended, axis=0)
    loads[4].wait()
    layer_one = (pts[...].astype(F32) + dot(attended_one, o1[...])).astype(BF16)
    pts[...] = layer_one
    normed_two = rms_round(layer_one.astype(F32))
    slots = dot(pack, normed_two).reshape(WIDE, SLOT, WIDTH).astype(BF16)
    snd[...] = slots
    rcv[0] = slots[0]

    def send_rows(k, g, dy, i):
        move(snd, rcv, k, fwd_send, fwd_recv.at[g], peer(dy, i)).start()

    each_slot(send_rows, order=[(j, i) for j in range(8) for i in (4, 5, 2, 6, 3, 7, 0, 1)])

    def arrived(src, dest, first, count, send_sem, recv_sem):
        return pltpu.make_async_remote_copy(
            src_ref=src.at[pl.ds(first, count)],
            dst_ref=dest.at[pl.ds(first, count)],
            send_sem=send_sem,
            recv_sem=recv_sem,
            device_id=(peer(0, 1), z),
            device_id_type=MESH,
        )

    def group(g):
        return (1, GSLOTS - 1) if g == 0 else (g * GSLOTS, GSLOTS)

    arrived(meta_s, meta_r, 1, WIDE - 1, meta_send, meta_recv).wait_recv()
    marks = meta_r[...].astype(F32).reshape(SLOTROWS, 128)
    lanes = iota((SLOTROWS, 128), 1)
    use = (lanes == 2) | (lanes == 3)
    query_mark = jnp.where(use, pltpu.roll(marks, 2, 1), 0.0).astype(BF16)
    key_mark = jnp.where(use, (1.0 - marks) * NEGATIVE, 0.0).astype(BF16)

    loads[5].wait()
    def project(g):
        first, count = group(g)
        arrived(snd, rcv, first, count, fwd_send, fwd_recv.at[g]).wait_recv()
        rows = rcv[g * GSLOTS : (g + 1) * GSLOTS].astype(F32).reshape(GROWS, WIDTH).astype(BF16)
        qkv2[g * GROWS : (g + 1) * GROWS, :] = dot(rows, w2[...]).astype(BF16)

    def scored(g, pair, keys):
        at = pair * 128
        mark = query_mark[g * GROWS : (g + 1) * GROWS]
        query = two_heads(qkv2[g * GROWS : (g + 1) * GROWS, at : at + 128] * 0.125)
        query = jnp.concatenate([query, jnp.concatenate([mark, mark], axis=0)], axis=1)
        key = jnp.concatenate([qkv2[keys, WIDTH + at : WIDTH + at + 128], key_mark[keys]], axis=1)
        return dot_t(query, key), qkv2[keys, 2 * WIDTH + at : 2 * WIDTH + at + 128]

    last = GROUPS - 1
    early, late = slice(0, last * GROWS), slice(last * GROWS, SLOTROWS)
    for g in range(last):
        project(g)
    begun_two = [[softmax_part(*scored(g, pair, early)) for pair in range(PAIRS)] for g in range(2)]
    project(last)

    for g in range(GROUPS):
        parts = []
        for pair in range(PAIRS):
            if g < 2:
                parts.append(softmax_rest(begun_two[g][pair], *scored(g, pair, late)))
            else:
                parts.append(both_heads(softmax_part(*scored(g, pair, slice(0, SLOTROWS)))[1]))
        mixture = jnp.concatenate(parts, axis=1).reshape(GSLOTS, SLOT, WIDTH).astype(BF16)
        bsnd[g * GSLOTS : (g + 1) * GSLOTS] = mixture
        if g == 0:
            brcv[0] = mixture[0]

        def send_back(k, g, dy, i):
            move(bsnd, brcv, k, back_send, back_recv.at[g], source(dy, i)).start()

        each_slot(send_back, (g,), [(j, i) for j in range(8) for i in (4, 5, 2, 6, 3, 7, 0, 1)])

    loads[6].wait()
    total = jnp.zeros((ROWS, WIDTH), F32)
    for g in range(GROUPS):
        first, count = group(g)
        arrived(bsnd, brcv, first, count, back_send, back_recv.at[g]).wait_recv()
        rows = brcv[g * GSLOTS : (g + 1) * GSLOTS].astype(F32).reshape(GROWS, WIDTH).astype(BF16)
        total = total + dot(unpack[:, g * GROWS : (g + 1) * GROWS], rows)
    out_ref[...] = (pts[...].astype(F32) + dot(total.astype(BF16), o2[...])).astype(BF16)

    for copy in sent:
        copy.wait_send()
    arrived(meta_s, meta_r, 1, WIDE - 1, meta_send, meta_recv).wait_send()
    arrived(snd, rcv, 1, WIDE - 1, fwd_send, fwd_recv.at[0]).wait_send()
    arrived(bsnd, brcv, 1, WIDE - 1, back_send, back_recv.at[0]).wait_send()


def on_device(points, counts, destination, rotated_ball, qkv_first, out_first, qkv_second, out_second):
    rows = points.reshape(ROWS, WIDTH)
    dma = pltpu.SemaphoreType.DMA
    hbm = pl.BlockSpec(memory_space=pltpu.MemorySpace.HBM)
    result = pl.pallas_call(
        kernel,
        out_shape=jax.ShapeDtypeStruct((ROWS, WIDTH), BF16),
        in_specs=[hbm] * 8,
        out_specs=pl.BlockSpec(memory_space=pltpu.VMEM),
        scratch_shapes=[
            pltpu.VMEM((ROWS, WIDTH), BF16),
            pltpu.VMEM((2, 32), jnp.int32),
            pltpu.VMEM((2, 32), jnp.int32),
            pltpu.VMEM((2, 32), jnp.int32),
            pltpu.VMEM((WIDTH, 3 * WIDTH), BF16),
            pltpu.VMEM((WIDTH, WIDTH), BF16),
            pltpu.VMEM((WIDTH, 3 * WIDTH), BF16),
            pltpu.VMEM((WIDTH, WIDTH), BF16),
            pltpu.VMEM((NZ, 2, BLOCKS // 2, WIDTH), BF16),
            pltpu.VMEM((WIDE, SLOT, 128), BF16),
            pltpu.VMEM((WIDE, SLOT, 128), BF16),
            pltpu.VMEM((WIDE, SLOT, WIDTH), BF16),
            pltpu.VMEM((WIDE, SLOT, WIDTH), BF16),
            pltpu.VMEM((WIDE, SLOT, WIDTH), BF16),
            pltpu.VMEM((WIDE, SLOT, WIDTH), BF16),
            pltpu.VMEM((ROWS, 3 * WIDTH), BF16),
            pltpu.VMEM((SLOTROWS, 3 * WIDTH), BF16),
            pltpu.VMEM((ROWS, SLOTROWS), BF16),
            dma((9,)),
            dma((NZ, 2)),
            dma((NZ, 2)),
            dma,
            dma,
            dma,
            dma((GROUPS,)),
            dma,
            dma((GROUPS,)),
        ],
        compiler_params=pltpu.CompilerParams(
            collective_id=0, has_side_effects=True, vmem_limit_bytes=48 * 1024 * 1024
        ),
    )(*[pltpu.with_memory_space_constraint(a, pltpu.HBM) for a in (rows, counts, destination, rotated_ball, qkv_first, out_first, qkv_second, out_second)])
    return result.reshape(points.shape)


def solution(mesh):
    in_specs = (
        P("wide", "narrow", None),
        P("wide", "narrow"),
        P("wide", "narrow"),
        P("wide", "narrow"),
        P(),
        P(),
        P(),
        P(),
    )
    out_specs = P("wide", "narrow", None)
    return jax.shard_map(
        on_device, mesh=mesh, in_specs=in_specs, out_specs=out_specs, check_vma=False
    )
```
